512 devices in a mesh: ctx: 64 (over z, y), tp: 8 (over x, core).
Axes of the slice: x: 4, y: 8, z: 8, core: 2. Of those that a mesh axis runs over, the one named last changes fastest.
Arguments:
- span_q: bfloat16 [8192, 8192], P('ctx', 'tp'), may hold values from -21 to 21
- span_kv: bfloat16 [2, 8192, 1024], P(None, 'ctx', 'tp'), may hold values from -20 to 20
- cache_kv: bfloat16 [2, 65536, 1024], P(None, 'ctx', 'tp'), may hold values from -20 to 20
- anchor_kv: bfloat16 [2, 2048, 1024], P(None, 'ctx', 'tp'), may hold values from -20 to 20
- block_len: int32 [64], P('ctx'), may hold values from 1 to 1024, 40960 in all
- queries: bfloat16 [128, 8192], P('ctx', 'tp'), may hold values from -21 to 21
- out_weight: bfloat16 [8192, 8192], P('tp', 'ctx'), may hold values from -0.0625 to 0.0625
Outputs:
- span_out: bfloat16 [8192, 8192], P('ctx', 'tp')
- answer: bfloat16 [128, 8192], P('tp', 'ctx')
The draws below stay inside these ranges and needn't reach their ends.
Inputs may be any that keep to these rules, and one draw needn't show every extreme that they name: The new tokens of block c follow its block_len[c] valid cache rows.
All inputs are finite; a program needn't handle non-finite values.
Results may differ from the reference program's by a relative error of at most 0.0049.
Values may be sent and summed in bfloat16 or wider, within the bound.
A program may use at most 64 MiB of HBM per device.

```python
import math
import jax
import jax.numpy as jnp
import numpy as np
from jax import lax

D = 8192
HEADS = 64
KVH = 8
HD = 128
QTOK = 128
SPAN = 128
BLK = 1024
ANC_DEV = 32
ANCHOR = 2048
SPAN_ROWS = 8192
CACHE_ROWS = 65536
N_CTX = 64


def base_noise(key, shape):
    return jnp.clip(jax.random.normal(key, shape, jnp.float32), -4.0, 4.0)


def kv_pair(key, row_count, salt):
    key_noise = base_noise(jax.random.fold_in(key, salt), (row_count, KVH * HD))
    key_scale = jnp.exp(jax.random.uniform(jax.random.fold_in(key, salt + 1), (row_count, 1), jnp.float32, jnp.log(0.5), jnp.log(5.0)))
    value_noise = base_noise(jax.random.fold_in(key, salt + 2), (row_count, KVH * HD))
    value_scale = jnp.exp(jax.random.uniform(jax.random.fold_in(key, salt + 3), (row_count, 1), jnp.float32, jnp.log(0.5), jnp.log(2.0)))
    return (key_noise * key_scale, value_noise * value_scale)


def drawn_queries(key, row_count, salt):
    values = base_noise(jax.random.fold_in(key, salt), (row_count, HEADS * HD))
    return values


def draw_anchor_kv(key, part):
    keys_part, values_part = kv_pair(key, ANCHOR, 10)
    return jnp.stack([keys_part, values_part]).astype(jnp.bfloat16)


def draw_cache_kv(key, part):
    keys_part, values_part = kv_pair(key, CACHE_ROWS, 20)
    return jnp.stack([keys_part, values_part]).astype(jnp.bfloat16)


def draw_span_kv(key, part):
    keys_part, values_part = kv_pair(key, SPAN_ROWS, 30)
    return jnp.stack([keys_part, values_part]).astype(jnp.bfloat16)


def draw_span_q(key, part):
    return drawn_queries(key, SPAN_ROWS, 40).astype(jnp.bfloat16)


def draw_queries(key, part):
    return drawn_queries(key, QTOK, 50).astype(jnp.bfloat16)


def block_levels(rng, extent, pieces, low, largest):
    def one(dim, blocks):
        heights = jax.random.uniform(jax.random.fold_in(jax.random.fold_in(rng, 6), dim), (blocks,), jnp.float32, low / len(pieces), largest / len(pieces))
        return jnp.repeat(jnp.exp(heights), extent[dim] // blocks).reshape((-1,) + (1,) * (len(extent) - dim - 1))

    gain = one(*pieces[0])
    for cut in pieces[1:]:
        gain = gain * one(*cut)
    return gain


def length_profile(amount, total, reach, lean):
    weights = [(1 << 20) // math.isqrt(standing ** lean) + 1 for standing in range(2, amount + 1)]
    spare, given = total - reach - (amount - 1), [1] * (amount - 1)
    while spare > 0:
        candidates = [i for i in range(amount - 1) if given[i] < reach]
        whole, left = sum([weights[i] for i in candidates]), spare
        for i in candidates:
            more = min(reach - given[i], max(1, left * weights[i] // whole), spare)
            given[i] = given[i] + more
            spare = spare - more
    return np.array([reach] + given)


def ragged_sizes(own_key, count, total, bound, slope):
    if count == 2:
        one = jax.random.randint(own_key, (), max(1, total - bound), min(bound, total - 1) + 1)
        return jnp.stack([one, total - one])
    tallies = jnp.asarray(length_profile(count, total, bound, slope), jnp.int32)
    pairs = (count - 1) // 2
    donor, receiver = tallies[1:1 + 2 * pairs:2], tallies[2:2 + 2 * pairs:2]
    slack = jnp.minimum(donor - 1, bound - receiver)
    passed = jax.random.randint(jax.random.fold_in(own_key, 1), (pairs,), 0, 1 << 20) % (slack + 1)
    tallies = tallies.at[1:1 + 2 * pairs:2].set(donor - passed).at[2:2 + 2 * pairs:2].set(receiver + passed)
    return tallies[jax.random.permutation(jax.random.fold_in(own_key, 2), count)]


def scatter_about(key, dims, width, most, split=(), kind=jnp.bfloat16):
    drawn = width * jax.random.normal(key, dims, jnp.float32)
    if split:
        drawn = drawn * block_levels(key, dims, split, -0.22, 0.18)
    return jnp.clip(drawn, -most, most).astype(kind)


def setup_inputs(seed: int = 0) -> dict:
    streams_of = jax.random.split(jax.random.key(seed), 8)
    return {
        "span_q": draw_span_q(jax.random.fold_in(streams_of[7], 71), 0),
        "span_kv": draw_span_kv(jax.random.fold_in(streams_of[7], 71), 0),
        "cache_kv": draw_cache_kv(jax.random.fold_in(streams_of[7], 71), 0),
        "anchor_kv": draw_anchor_kv(jax.random.fold_in(streams_of[7], 71), 0),
        "block_len": ragged_sizes(streams_of[4], N_CTX, N_CTX * BLK * 5 // 8, BLK, 2).astype(jnp.int32),
        "queries": draw_queries(jax.random.fold_in(streams_of[7], 71), 0),
        "out_weight": scatter_about(streams_of[6], (HEADS * HD, D), (HEADS * HD) ** -0.5, 0.0625, ((0, 8), (1, 64))),
    }


masked_score = -1e+30

def block_softmax(query_rows, key_rows, value_rows, visible):
    scores = jnp.einsum('rkgd,nkd->rkgn', query_rows, key_rows, precision=lax.Precision.HIGHEST) * (1.0 / math.sqrt(HD))
    scores = jnp.where(visible[:, None, None, :], scores, masked_score)
    row_max = lax.optimization_barrier(jnp.max(scores, axis=3))
    weights = jnp.exp(scores - row_max[..., None])
    row_sum = lax.optimization_barrier(jnp.sum(weights, axis=3))
    rounded = lax.optimization_barrier(weights.astype(jnp.bfloat16)).astype(jnp.float32)
    summed = jnp.einsum('rkgn,nkd->rkgd', rounded, value_rows, precision=lax.Precision.HIGHEST)
    return (row_max, row_sum, summed)

def reference(span_q, span_kv, cache_kv, anchor_kv, block_len, queries, out_weight):
    group_size = HEADS // KVH
    anchor_full = anchor_kv.astype(jnp.float32).reshape(2, ANCHOR, KVH, HD)

    def first_block(block_index):
        q_rows = lax.dynamic_slice_in_dim(span_q, block_index * SPAN, SPAN, 0)
        q_rows = q_rows.astype(jnp.float32).reshape(SPAN, KVH, group_size, HD)
        cache_piece = lax.dynamic_slice_in_dim(cache_kv, block_index * BLK, BLK, 1)
        cache_piece = cache_piece.astype(jnp.float32).reshape(2, BLK, KVH, HD)
        span_piece = lax.dynamic_slice_in_dim(span_kv, block_index * SPAN, SPAN, 1)
        span_piece = span_piece.astype(jnp.float32).reshape(2, SPAN, KVH, HD)
        key_rows = jnp.concatenate([anchor_full[0], cache_piece[0], span_piece[0]], axis=0)
        value_rows = jnp.concatenate([anchor_full[1], cache_piece[1], span_piece[1]], axis=0)
        length = lax.dynamic_index_in_dim(block_len, block_index, keepdims=False)
        count_all = ANCHOR + BLK + SPAN
        column = lax.broadcasted_iota(jnp.int32, (SPAN, count_all), 1)
        query_pos = lax.broadcasted_iota(jnp.int32, (SPAN, count_all), 0)
        in_cache = (column >= ANCHOR) & (column < ANCHOR + BLK)
        in_span = column >= ANCHOR + BLK
        visible = jnp.where(in_cache, column - ANCHOR < length, jnp.where(in_span, column - ANCHOR - BLK <= query_pos, True))
        row_max, row_sum, summed = block_softmax(q_rows, key_rows, value_rows, visible)
        return (summed / row_sum[..., None]).reshape(SPAN, HEADS * HD).astype(jnp.bfloat16)
    block_ids = jnp.arange(N_CTX, dtype=jnp.int32)
    span_out = lax.map(first_block, block_ids).reshape(SPAN_ROWS, HEADS * HD)
    query_all = queries.astype(jnp.float32).reshape(QTOK, KVH, group_size, HD)

    def second_block(block_index):
        anchor_piece = lax.dynamic_slice_in_dim(anchor_kv, block_index * ANC_DEV, ANC_DEV, 1)
        anchor_piece = anchor_piece.astype(jnp.float32).reshape(2, ANC_DEV, KVH, HD)
        cache_piece = lax.dynamic_slice_in_dim(cache_kv, block_index * BLK, BLK, 1)
        cache_piece = cache_piece.astype(jnp.float32).reshape(2, BLK, KVH, HD)
        span_piece = lax.dynamic_slice_in_dim(span_kv, block_index * SPAN, SPAN, 1)
        span_piece = span_piece.astype(jnp.float32).reshape(2, SPAN, KVH, HD)
        key_rows = jnp.concatenate([anchor_piece[0], cache_piece[0], span_piece[0]], axis=0)
        value_rows = jnp.concatenate([anchor_piece[1], cache_piece[1], span_piece[1]], axis=0)
        length = lax.dynamic_index_in_dim(block_len, block_index, keepdims=False)
        column = lax.broadcasted_iota(jnp.int32, (1, ANC_DEV + BLK + SPAN), 1)
        in_cache = (column >= ANC_DEV) & (column < ANC_DEV + BLK)
        visible = jnp.where(in_cache, column - ANC_DEV < length, True)
        return block_softmax(query_all, key_rows, value_rows, visible)
    part_max, part_sum, part_values = lax.map(second_block, block_ids)
    global_max = lax.optimization_barrier(jnp.max(part_max, axis=0))
    rescale = jnp.exp(part_max - global_max[None])
    total_sum = lax.optimization_barrier(jnp.sum(rescale * part_sum, axis=0))
    total_values = lax.optimization_barrier(jnp.sum(rescale[..., None] * part_values, axis=0))
    attended = (total_values / total_sum[..., None]).reshape(QTOK, HEADS * HD).astype(jnp.bfloat16)
    answer = jnp.dot(attended, out_weight, preferred_element_type=jnp.float32).astype(jnp.bfloat16)
    return (span_out, answer)
```

```python
import math

import jax
import jax.numpy as jnp
from jax import lax
from jax.experimental import pallas as pl
from jax.experimental.pallas import tpu as pltpu
from jax.sharding import PartitionSpec as P

HD = 128
NEG = -1e30
MESH = pl.DeviceIdType.MESH
LOG2 = math.log2(math.e) / math.sqrt(HD)

QA, QB, AB, AA, RO, RL, CO, CL, GB, TP = range(10)


def scores(q, k):
    return lax.dot_general(q, k, (((1,), (1,)), ((), ())), preferred_element_type=jnp.float32)


def softmax_parts(parts, values):
    peak = None
    for s in parts:
        top = jnp.max(s, axis=1, keepdims=True)
        peak = top if peak is None else jnp.maximum(peak, top)
    total, out = None, None
    for s, v in zip(parts, values):
        w = jnp.exp2((s - peak) * LOG2)
        part = jnp.sum(w, axis=1, keepdims=True)
        prod = jnp.dot(w.astype(jnp.bfloat16), v, preferred_element_type=jnp.float32)
        total = part if total is None else total + part
        out = prod if out is None else out + prod
    return peak, total, out


def make_kernel(side, nt, heads):
    ctx_count = side * side

    def kernel(
        len_ref, span_q_hbm, span_kv_hbm, cache_hbm, anchor_hbm, queries_hbm, weight_hbm,
        span_out_hbm, answer_hbm,
        span_q, span_kv, cache, anchor, queries, weight, q_rows, bias,
        q_all, anc, ro_send, rl_send, ro, rl, co, cl, att, att_f, proj, tpr, out, ans,
        in_sem, ss, rs, out_sem,
    ):
        rows = q_all.shape[1] * q_all.shape[2]
        ctx = lax.axis_index("ctx")
        t = lax.axis_index("tp")
        par = lax.rem(t, 2)
        lo, hi = lax.rem(ctx, side), lax.div(ctx, side)
        a = lo + par * (hi - lo)
        b = hi + par * (lo - hi)

        def at(pa, pb):
            first = pb * side + pa
            return {"ctx": first + par * (pa * side + pb - first)}

        def on_a(k):
            return at(lax.rem(a + k, side), b)

        def on_b(k):
            return at(a, lax.rem(b + k, side))

        def on_t(k):
            return {"tp": lax.rem(t + k, nt)}

        def rcopy(src, dst, x, k, dev):
            return pltpu.make_async_remote_copy(
                src_ref=src, dst_ref=dst, send_sem=ss.at[x, k], recv_sem=rs.at[x, k],
                device_id=dev, device_id_type=MESH,
            )

        loads = [
            pltpu.make_async_copy(src, dst, in_sem.at[i])
            for i, (src, dst) in enumerate(
                (
                    (queries_hbm, queries), (anchor_hbm, anchor), (cache_hbm, cache),
                    (span_kv_hbm, span_kv), (span_q_hbm, span_q), (weight_hbm, weight),
                )
            )
        ]
        for load in loads:
            load.start()
        barrier = pltpu.get_barrier_semaphore()
        for k in range(1, side):
            pl.semaphore_signal(barrier, inc=1, device_id=on_a(k), device_id_type=MESH)
            pl.semaphore_signal(barrier, inc=1, device_id=on_b(k), device_id_type=MESH)
        for k in range(1, nt):
            pl.semaphore_signal(barrier, inc=1, device_id=on_t(k), device_id_type=MESH)

        loads[0].wait()
        loads[1].wait()
        wide = queries[...].astype(jnp.float32)
        for i in range(queries.shape[0]):
            for h in range(heads):
                q_rows[i * heads + h : i * heads + h + 1, :] = wide[i : i + 1, h * HD : (h + 1) * HD]
        q_all[b, a] = q_rows[...].astype(jnp.bfloat16)
        own_rows = anchor.shape[1]
        anc[a, :, pl.ds(b * own_rows, own_rows), :] = anchor[...]
        length = len_ref[0]
        column = lax.broadcasted_iota(jnp.int32, bias.shape, 1)
        bias[...] = jnp.where(column < length, 0.0, NEG)

        pl.semaphore_wait(barrier, 2 * (side - 1) + nt - 1)

        far_first = sorted(range(1, side), key=lambda k: -min(k, side - k))

        def qa(k, owner):
            return rcopy(q_all.at[b, owner], q_all.at[b, owner], QA, k, on_a(k))

        def qb(k, owner):
            return rcopy(q_all.at[owner], q_all.at[owner], QB, k, on_b(k))

        def ab(k, owner):
            place = anc.at[a, :, pl.ds(owner * own_rows, own_rows), :]
            return rcopy(place, place, AB, k, on_b(k))

        def aa(k, owner):
            return rcopy(anc.at[owner], anc.at[owner], AA, k, on_a(k))

        for k in far_first:
            qa(k, a).start()
        for k in far_first:
            ab(k, b).start()
        for load in loads[2:]:
            load.wait()
        for k in far_first:
            qa(k, lax.rem(a + side - k, side)).wait_recv()
        for k in far_first:
            qb(k, b).start()
        for k in far_first:
            ab(k, lax.rem(b + side - k, side)).wait_recv()
        for k in far_first:
            aa(k, a).start()

        diag = lax.broadcasted_iota(jnp.int32, (rows, rows), 0) == lax.broadcasted_iota(
            jnp.int32, (rows, rows), 1
        )

        def as_row(col):
            return jnp.sum(jnp.where(diag, col, 0.0), axis=0, keepdims=True)

        def as_col(row):
            return jnp.sum(jnp.where(diag, row, 0.0), axis=1, keepdims=True)

        def query_block(owner, o_ref, l_ref):
            q = q_all[owner].reshape(rows, HD)
            parts = [
                scores(q, cache[0]) + bias[0:1, :],
                scores(q, span_kv[0]),
                scores(q, anchor[0]),
            ]
            peak, total, o = softmax_parts(parts, [cache[1], span_kv[1], anchor[1]])
            o_ref[...] = (o / total).astype(jnp.bfloat16)
            lse = as_row(peak * LOG2 + jnp.log2(total))
            l_ref[...] = jnp.broadcast_to(lse, l_ref.shape)

        query_block(b, ro.at[b], rl.at[b])

        def ro_copy(k, src, owner):
            return rcopy(src, ro.at[owner], RO, k, on_b(k))

        def rl_copy(k, src, owner):
            return rcopy(src, rl.at[owner], RL, k, on_b(k))

        def one_block(i, carry):
            k = lax.rem(i, 2) * lax.div(i + 1, 2) + (1 - lax.rem(i, 2)) * (side - lax.div(i, 2))
            owner = lax.rem(b + side - k, side)
            qb(k, owner).wait_recv()
            query_block(owner, ro_send.at[owner], rl_send.at[owner])
            back = side - k
            ro_copy(back, ro_send.at[owner], b).start()
            rl_copy(back, rl_send.at[owner], b).start()
            return carry

        lax.fori_loop(1, side, one_block, 0)

        def combine(o_ref, l_ref):
            lse = [l_ref[i, 0:1, :] for i in range(side)]
            peak = lse[0]
            for x in lse[1:]:
                peak = jnp.maximum(peak, x)
            weights = [jnp.exp2(x - peak) for x in lse]
            total = weights[0]
            for w in weights[1:]:
                total = total + w
            o = None
            for i in range(side):
                term = as_col(weights[i] / total) * o_ref[i].astype(jnp.float32)
                o = term if o is None else o + term
            return o.astype(jnp.bfloat16), peak + jnp.log2(total)

        for k in range(1, side):
            owner = lax.rem(b + side - k, side)
            ro_copy(k, ro_send.at[owner], owner).wait_recv()
            rl_copy(k, rl_send.at[owner], owner).wait_recv()
        o, lse = combine(ro, rl)
        co[a] = o
        cl[a] = jnp.broadcast_to(lse, cl.shape[1:])

        def co_copy(k, owner):
            return rcopy(co.at[owner], co.at[owner], CO, k, on_a(k))

        def cl_copy(k, owner):
            return rcopy(cl.at[owner], cl.at[owner], CL, k, on_a(k))

        for k in far_first:
            co_copy(k, a).start()
            cl_copy(k, a).start()

        for k in range(1, side):
            aa(k, lax.rem(a + side - k, side)).wait_recv()
        new_rows = span_q.shape[0]
        causal = lax.broadcasted_iota(jnp.int32, (new_rows, new_rows), 1) <= lax.broadcasted_iota(
            jnp.int32, (new_rows, new_rows), 0
        )

        def one_head(h, carry):
            cols = pl.ds(pl.multiple_of(h * HD, HD), HD)
            q = span_q[:, cols]
            anc_k = anc[:, 0].reshape(-1, HD)
            anc_v = anc[:, 1].reshape(-1, HD)
            parts = [
                scores(q, anc_k),
                scores(q, cache[0]) + bias[0:1, :],
                jnp.where(causal, scores(q, span_kv[0]), NEG),
            ]
            _, total, o = softmax_parts(parts, [anc_v, cache[1], span_kv[1]])
            out[:, cols] = (o / total).astype(jnp.bfloat16)
            return carry

        lax.fori_loop(0, heads // 2, one_head, 0)

        for k in range(1, side):
            owner = lax.rem(a + side - k, side)
            co_copy(k, owner).wait_recv()
            cl_copy(k, owner).wait_recv()
        o, _ = combine(co, cl)
        att[b] = o

        def gb(k, owner):
            return rcopy(att.at[owner], att.at[owner], GB, k, on_b(k))

        for k in far_first:
            gb(k, b).start()

        lax.fori_loop(heads // 2, heads, one_head, 0)
        store = pltpu.make_async_copy(out, span_out_hbm, out_sem.at[0])
        store.start()

        for k in range(1, side):
            gb(k, lax.rem(b + side - k, side)).wait_recv()
        att_f[...] = att[...].reshape(-1, HD).astype(jnp.float32)
        count = att_f.shape[0] // heads
        per = count // ctx_count
        row = lax.broadcasted_iota(jnp.int32, (count, count), 0)
        col = lax.broadcasted_iota(jnp.int32, (count, count), 1)
        dev, sub = lax.div(row, per), lax.rem(row, per)
        swapped = (lax.rem(dev, side) * side + lax.div(dev, side)) * per + sub
        source = row + par * (swapped - row)
        perm = jnp.where(col == source, 1.0, 0.0).astype(jnp.bfloat16)
        total = None
        for h in range(heads):
            rows_h = att_f[pl.ds(h, count, stride=heads), :].astype(jnp.bfloat16)
            rows_h = jnp.dot(perm, rows_h, preferred_element_type=jnp.float32)
            term = jnp.dot(
                rows_h.astype(jnp.bfloat16), weight[h * HD : (h + 1) * HD, :],
                preferred_element_type=jnp.float32,
            )
            total = term if total is None else total + term
        proj[...] = total.reshape(proj.shape)
        tpr[t] = proj[t]

        def tp_copy(k, piece, owner):
            return rcopy(proj.at[piece], tpr.at[owner], TP, k, on_t(k))

        for k in range(1, nt):
            tp_copy(k, lax.rem(t + k, nt), t).start()
        for k in range(1, nt):
            owner = lax.rem(t + nt - k, nt)
            tp_copy(k, owner, owner).wait_recv()
        total = tpr[0]
        for i in range(1, nt):
            total = total + tpr[i]
        ans[...] = total.astype(jnp.bfloat16)
        final = pltpu.make_async_copy(ans, answer_hbm, out_sem.at[1])
        final.start()

        for k in range(1, side):
            peer = lax.rem(b + k, side)
            qa(k, a).wait_send()
            qb(k, b).wait_send()
            ab(k, b).wait_send()
            aa(k, a).wait_send()
            ro_copy(k, ro_send.at[peer], b).wait_send()
            rl_copy(k, rl_send.at[peer], b).wait_send()
            co_copy(k, a).wait_send()
            cl_copy(k, a).wait_send()
            gb(k, b).wait_send()
        for k in range(1, nt):
            tp_copy(k, lax.rem(t + k, nt), t).wait_send()
        store.wait()
        final.wait()

    return kernel


def make_local(ctx_count, nt):
    side = math.isqrt(ctx_count)

    def local(span_q, span_kv, cache_kv, anchor_kv, block_len, queries, out_weight):
        heads = span_q.shape[1] // HD
        per = queries.shape[0]
        chunk = per * heads
        rows = side * chunk
        own = anchor_kv.shape[1]
        cols = out_weight.shape[1]
        answer_rows = per * ctx_count // nt
        any_spec = pl.BlockSpec(memory_space=pl.ANY)
        bf16, f32 = jnp.bfloat16, jnp.float32
        vmem = pltpu.VMEM
        return pl.pallas_call(
            make_kernel(side, nt, heads),
            name="star",
            out_shape=(
                jax.ShapeDtypeStruct(span_q.shape, bf16),
                jax.ShapeDtypeStruct((answer_rows, cols), bf16),
            ),
            in_specs=[pl.BlockSpec(memory_space=pltpu.SMEM)] + [any_spec] * 6,
            out_specs=(any_spec, any_spec),
            scratch_shapes=[
                vmem(span_q.shape, bf16),
                vmem(span_kv.shape, bf16),
                vmem(cache_kv.shape, bf16),
                vmem(anchor_kv.shape, bf16),
                vmem(queries.shape, bf16),
                vmem(out_weight.shape, bf16),
                vmem((chunk, HD), f32),
                vmem((8, cache_kv.shape[1]), f32),
                vmem((side, side, chunk, HD), bf16),
                vmem((side, 2, side * own, HD), bf16),
                vmem((side, rows, HD), bf16),
                vmem((side, 8, rows), f32),
                vmem((side, rows, HD), bf16),
                vmem((side, 8, rows), f32),
                vmem((side, rows, HD), bf16),
                vmem((side, 8, rows), f32),
                vmem((side, rows, HD), bf16),
                vmem((side * rows, HD), f32),
                vmem((nt, answer_rows, cols), f32),
                vmem((nt, answer_rows, cols), f32),
                vmem(span_q.shape, bf16),
                vmem((answer_rows, cols), bf16),
                pltpu.SemaphoreType.DMA((6,)),
                pltpu.SemaphoreType.DMA((10, 8)),
                pltpu.SemaphoreType.DMA((10, 8)),
                pltpu.SemaphoreType.DMA((2,)),
            ],
            compiler_params=pltpu.CompilerParams(collective_id=0, has_side_effects=True),
        )(block_len, span_q, span_kv, cache_kv, anchor_kv, queries, out_weight)

    return local


def solution(mesh):
    placed = (
        P("ctx", "tp"),
        P(None, "ctx", "tp"),
        P(None, "ctx", "tp"),
        P(None, "ctx", "tp"),
        P("ctx"),
        P("ctx", "tp"),
        P("tp", "ctx"),
    )
    return jax.shard_map(
        make_local(mesh.shape["ctx"], mesh.shape["tp"]),
        mesh=mesh,
        in_specs=placed,
        out_specs=(P("ctx", "tp"), P("tp", "ctx")),
        check_vma=False,
    )
```

```python
import math

import jax
import jax.numpy as jnp
from jax import lax
from jax.experimental import pallas as pl
from jax.experimental.pallas import tpu as pltpu
from jax.sharding import PartitionSpec as P

HD = 128
NEG = -1e30
MESH = pl.DeviceIdType.MESH
LOG2 = math.log2(math.e) / math.sqrt(HD)

QA, QB, AB, AA, RO, RL, CO, CL, GB, TP = range(10)


def scores(q, k):
    return lax.dot_general(q, k, (((1,), (1,)), ((), ())), preferred_element_type=jnp.float32)


def softmax_parts(parts, values):
    peak = None
    for s in parts:
        top = jnp.max(s, axis=1, keepdims=True)
        peak = top if peak is None else jnp.maximum(peak, top)
    total, out = None, None
    for s, v in zip(parts, values):
        w = jnp.exp2((s - peak) * LOG2)
        part = jnp.sum(w, axis=1, keepdims=True)
        prod = jnp.dot(w.astype(jnp.bfloat16), v, preferred_element_type=jnp.float32)
        total = part if total is None else total + part
        out = prod if out is None else out + prod
    return peak, total, out


def wide(x, columns):
    return x if columns == x.shape[1] else jnp.concatenate([x] * (columns // x.shape[1]), axis=1)


def lane_softmax(parts, values, before=None):
    top = None
    for s in parts:
        for c in range(0, s.shape[1], HD):
            piece = s[:, c : c + HD]
            top = piece if top is None else jnp.maximum(top, piece)
    peak = jnp.broadcast_to(jnp.max(top, axis=1, keepdims=True), top.shape)
    if before is not None:
        peak = jnp.maximum(peak, before)
    total, out = None, None
    for s, v in zip(parts, values):
        w = jnp.exp2((s - wide(peak, s.shape[1])) * LOG2)
        for c in range(0, w.shape[1], HD):
            piece = w[:, c : c + HD]
            total = piece if total is None else total + piece
        prod = jnp.dot(w.astype(jnp.bfloat16), v, preferred_element_type=jnp.float32)
        out = prod if out is None else out + prod
    return peak, total, out


def make_kernel(side, nt, heads):
    ctx_count = side * side
    half = side // 2

    def kernel(
        len_hbm, span_q_hbm, span_kv_hbm, cache_hbm, anchor_hbm, queries_hbm, weight_hbm,
        out, ans,
        len_ref, span_q, span_kv, cache, anchor, queries, weight, q_rows, bias,
        mine, qx, q_all, anc, ro_send, rl_send, ro, rl, co, cl, done, att, att_f, proj, tpr,
        f_peak, f_sum, f_out,
        in_sem, ss, rs,
    ):
        rows = q_all.shape[1] * q_all.shape[2]
        ctx = lax.axis_index("ctx")
        t = lax.axis_index("tp")
        par = lax.rem(t, 2)
        lo, hi = lax.rem(ctx, side), lax.div(ctx, side)
        a = lo + par * (hi - lo)
        b = hi + par * (lo - hi)

        other = t + 1 - 2 * par

        def at(pa, pb, core):
            first = pb * side + pa
            return {"ctx": first + par * (pa * side + pb - first), "tp": core}

        def on_a(k):
            return at(lax.rem(a + k, side), b, t)

        def on_b(k):
            return at(a, lax.rem(b + k, side), t)

        def over_a(k):
            return at(lax.rem(a + k, side), b, other)

        def over_b(k):
            return at(a, lax.rem(b + k, side), other)

        def back(x, k):
            return lax.rem(x + side - k, side)

        def on_t(k):
            return {"tp": lax.rem(t + k, nt)}

        def rcopy(src, dst, x, k, dev):
            return pltpu.make_async_remote_copy(
                src_ref=src, dst_ref=dst, send_sem=ss.at[x, k], recv_sem=rs.at[x, k],
                device_id=dev, device_id_type=MESH,
            )

        new_rows = out.shape[0]
        pairs = [
            (queries_hbm, queries), (anchor_hbm, anchor), (len_hbm, len_ref), (cache_hbm, cache),
            (span_kv_hbm, span_kv), (weight_hbm, weight),
        ]
        for h in range(heads):
            pairs.append(
                (span_q_hbm.at[:, h * HD : (h + 1) * HD], span_q.at[h * new_rows : (h + 1) * new_rows])
            )
        loads = [
            pltpu.make_async_copy(src, dst, in_sem.at[i]) for i, (src, dst) in enumerate(pairs)
        ]
        barrier = pltpu.get_barrier_semaphore()
        for k in range(1, side):
            for peer in (on_a(k), on_b(k), over_a(k), over_b(k)):
                pl.semaphore_signal(barrier, inc=1, device_id=peer, device_id_type=MESH)
        for k in range(1, nt):
            pl.semaphore_signal(barrier, inc=1, device_id=on_t(k), device_id_type=MESH)

        for load in loads:
            load.start()

        loads[0].wait()
        loads[1].wait()
        wide = queries[...].astype(jnp.float32)
        for i in range(queries.shape[0]):
            for h in range(heads):
                q_rows[i * heads + h : i * heads + h + 1, :] = wide[i : i + 1, h * HD : (h + 1) * HD]
        mine[...] = q_rows[...].astype(jnp.bfloat16)
        own_rows = anchor.shape[1]
        anc[b, :, pl.ds(a * own_rows, own_rows), :] = anchor[...]
        loads[2].wait()
        length = len_ref[0]
        column = lax.broadcasted_iota(jnp.int32, bias.shape, 1)
        bias[...] = jnp.where(column < length, 0.0, NEG)

        pl.semaphore_wait(barrier, 4 * (side - 1) + nt - 1)

        far_first = sorted(range(1, side), key=lambda k: -min(k, side - k))
        far_all = far_first + [0]

        def qa(k, owner):
            return rcopy(mine, qx.at[owner], QA, k, over_a(k))

        def qb_chunk(k, chunk):
            return rcopy(qx.at[chunk], q_all.at[a, chunk], QB, k, over_a(k))

        def qb(k, owner):
            return rcopy(qx, q_all.at[owner], QB, k, over_a(k))

        def ab(k, owner):
            place = anc.at[b, :, pl.ds(owner * own_rows, own_rows), :]
            return rcopy(place, place, AB, k, on_a(k))

        def right(step, slot):
            return rcopy(anc.at[slot], anc.at[slot], AA, step - 1, on_b(1))

        def left(step, slot):
            return rcopy(anc.at[slot], anc.at[slot], AA, half + step - 1, on_b(side - 1))

        def slot_at(offset):
            return lax.rem(b + side + offset, side)

        def ring_send(step):
            if step <= half:
                right(step, slot_at(1 - step)).start()
            if step <= half - 1:
                left(step, slot_at(step - 1)).start()

        def ring_recv(step):
            got = []
            if step <= half:
                got.append(slot_at(-step))
                right(step, got[-1]).wait_recv()
            if step <= half - 1:
                got.append(slot_at(step))
                left(step, got[-1]).wait_recv()
            return got

        for k in far_all:
            qa(k, a).start()
        for k in far_first:
            ab(k, a).start()

        group = min(heads, 4) * new_rows
        tri_row = lax.rem(lax.broadcasted_iota(jnp.int32, (group, new_rows), 0), new_rows)
        tri_col = lax.broadcasted_iota(jnp.int32, (group, new_rows), 1)

        def first_local(i, carry):
            r = pl.ds(pl.multiple_of(i * group, group), group)
            q = span_q[r, :]
            parts = [
                scores(q, cache[0]) + bias[0:1, :],
                jnp.where(tri_col <= tri_row, scores(q, span_kv[0]), NEG),
            ]
            peak, total, o = lane_softmax(parts, [cache[1], span_kv[1]])
            f_peak[r, :] = peak
            f_sum[r, :] = total
            f_out[r, :] = o
            return carry

        def first_anchor(slots, last=False):
            def body(i, carry):
                r = pl.ds(pl.multiple_of(i * group, group), group)
                q = span_q[r, :]
                parts = [scores(q, anc[s, 0]) for s in slots]
                before = f_peak[r, :]
                peak, total, o = lane_softmax(parts, [anc[s, 1] for s in slots], before)
                shrink = jnp.exp2((before - peak) * LOG2)
                total = f_sum[r, :] * shrink + total
                o = f_out[r, :] * shrink + o
                if last:
                    f_out[r, :] = o / jnp.sum(total, axis=1, keepdims=True)
                else:
                    f_peak[r, :] = peak
                    f_sum[r, :] = total
                    f_out[r, :] = o
                return carry

            lax.fori_loop(0, heads * new_rows // group, body, 0)

        for load in loads[3:]:
            load.wait()
        def forward(offsets):
            for d in offsets:
                chunk = back(b, d)
                qa(d, chunk).wait_recv()
                for k in far_all:
                    qb_chunk(k, chunk).start()

        groups = heads * new_rows // group
        lax.fori_loop(0, (groups + 1) // 2, first_local, 0)
        forward([0] + sorted({1, side - 1}))
        lax.fori_loop((groups + 1) // 2, groups, first_local, 0)
        for d in range(2, half + 1):
            forward(sorted({d, side - d}))
        for k in far_first:
            ab(k, back(a, k)).wait_recv()
        ring_send(1)

        diag = lax.broadcasted_iota(jnp.int32, (rows, rows), 0) == lax.broadcasted_iota(
            jnp.int32, (rows, rows), 1
        )

        def as_row(col):
            return jnp.sum(jnp.where(diag, col, 0.0), axis=0, keepdims=True)

        def as_col(row):
            return jnp.sum(jnp.where(diag, row, 0.0), axis=1, keepdims=True)

        def query_block(owner, o_ref, l_ref):
            q = q_all[owner].reshape(rows, HD)
            parts = [
                scores(q, cache[0]) + bias[0:1, :],
                scores(q, span_kv[0]),
                scores(q, anchor[0]),
            ]
            peak, total, o = softmax_parts(parts, [cache[1], span_kv[1], anchor[1]])
            o_ref[...] = (o / total).astype(jnp.bfloat16)
            l_ref[...] = as_row(peak * LOG2 + jnp.log2(total))

        def ro_copy(k, block, owner):
            return rcopy(ro_send.at[block], ro.at[owner], RO, k, over_b(k))

        def rl_copy(k, block, owner):
            return rcopy(rl_send.at[block], rl.at[owner], RL, k, over_b(k))

        def some_blocks(offsets):
            owners = [back(b, k) for k in offsets]
            for k, owner in zip(offsets, owners):
                qb(k, owner).wait_recv()
            for owner in owners:
                query_block(owner, ro_send.at[owner], rl_send.at[owner])
            for k, owner in zip(offsets, owners):
                k = lax.rem(side - k, side)
                ro_copy(k, owner, b).start()
                rl_copy(k, owner, b).start()

        some_blocks([0])


        def two_blocks(i, carry):
            some_blocks([i, side - i])
            return carry

        lax.fori_loop(1, half, two_blocks, 0)
        some_blocks([half])

        slots = [b] + ring_recv(1)
        ring_send(2)
        first_anchor(slots, last=half == 1)

        def combine(o_ref, l_ref):
            lse = [l_ref[i] for i in range(side)]
            peak = lse[0]
            for x in lse[1:]:
                peak = jnp.maximum(peak, x)
            weights = [jnp.exp2(x - peak) for x in lse]
            total = weights[0]
            for w in weights[1:]:
                total = total + w
            o = None
            for i in range(side):
                term = as_col(weights[i] / total) * o_ref[i].astype(jnp.float32)
                o = term if o is None else o + term
            return o.astype(jnp.bfloat16), peak + jnp.log2(total)

        for k in range(side):
            ro_copy(k, 0, back(a, k)).wait_recv()
            rl_copy(k, 0, back(a, k)).wait_recv()
        o, lse = combine(ro, rl)
        co[b] = o
        cl[b] = lse

        def co_copy(k, owner):
            return rcopy(co.at[owner], co.at[owner], CO, k, on_b(k))

        def cl_copy(k, owner):
            return rcopy(cl.at[owner], cl.at[owner], CL, k, on_b(k))

        for k in far_first:
            co_copy(k, b).start()
            cl_copy(k, b).start()

        if half > 1:
            slots = ring_recv(2)
            ring_send(3)
            first_anchor(slots, last=half == 2)
        for k in range(1, side):
            co_copy(k, back(b, k)).wait_recv()
            cl_copy(k, back(b, k)).wait_recv()
        o, _ = combine(co, cl)
        done[...] = o

        def gb(k, owner):
            return rcopy(done, att.at[owner], GB, k, over_a(k))

        for k in far_all:
            gb(k, a).start()

        for step in range(3, half):
            slots = ring_recv(step)
            ring_send(step + 1)
            first_anchor(slots)

        for k in range(side):
            gb(k, back(b, k)).wait_recv()
        att_f[...] = att[...].reshape(-1, HD).astype(jnp.float32)
        count = att_f.shape[0] // heads
        per = count // ctx_count
        row = lax.broadcasted_iota(jnp.int32, (count, count), 0)
        col = lax.broadcasted_iota(jnp.int32, (count, count), 1)
        dev, sub = lax.div(row, per), lax.rem(row, per)
        swapped = (lax.rem(dev, side) * side + lax.div(dev, side)) * per + sub
        source = row + par * (swapped - row)
        perm = jnp.where(col == source, 1.0, 0.0).astype(jnp.bfloat16)
        total = None
        for h in range(heads):
            rows_h = att_f[pl.ds(h, count, stride=heads), :].astype(jnp.bfloat16)
            rows_h = jnp.dot(perm, rows_h, preferred_element_type=jnp.float32)
            term = jnp.dot(
                rows_h.astype(jnp.bfloat16), weight[h * HD : (h + 1) * HD, :],
                preferred_element_type=jnp.float32,
            )
            total = term if total is None else total + term
        proj[...] = total.reshape(proj.shape)
        tpr[t] = proj[t]

        def tp_copy(k, piece, owner):
            return rcopy(proj.at[piece], tpr.at[owner], TP, k, on_t(k))

        for k in range(1, nt):
            tp_copy(k, lax.rem(t + k, nt), t).start()

        if half > 2:
            slots = ring_recv(half)
            first_anchor(slots, last=True)
        for h in range(heads):
            out[:, h * HD : (h + 1) * HD] = f_out[h * new_rows : (h + 1) * new_rows, :].astype(jnp.bfloat16)

        for k in range(1, nt):
            owner = lax.rem(t + nt - k, nt)
            tp_copy(k, owner, owner).wait_recv()
        total = tpr[0]
        for i in range(1, nt):
            total = total + tpr[i]
        ans[...] = total.astype(jnp.bfloat16)

        for step in range(1, half + 1):
            right(step, slot_at(1 - step)).wait_send()
            if step < half:
                left(step, slot_at(step - 1)).wait_send()
        for k in range(side):
            qa(k, a).wait_send()
            qb(k, a).wait_send()
            ro_copy(k, 0, b).wait_send()
            rl_copy(k, 0, b).wait_send()
            gb(k, a).wait_send()
        for k in range(1, side):
            ab(k, a).wait_send()
            co_copy(k, b).wait_send()
            cl_copy(k, b).wait_send()
        for k in range(1, nt):
            tp_copy(k, lax.rem(t + k, nt), t).wait_send()

    return kernel


def make_local(ctx_count, nt):
    side = math.isqrt(ctx_count)

    def local(span_q, span_kv, cache_kv, anchor_kv, block_len, queries, out_weight):
        new_rows = span_q.shape[0]
        heads = span_q.shape[1] // HD
        per = queries.shape[0]
        chunk = per * heads
        rows = side * chunk
        own = anchor_kv.shape[1]
        cols = out_weight.shape[1]
        answer_rows = per * ctx_count // nt
        any_spec = pl.BlockSpec(memory_space=pl.ANY)
        vmem_spec = pl.BlockSpec(memory_space=pltpu.VMEM)
        bf16, f32 = jnp.bfloat16, jnp.float32
        vmem = pltpu.VMEM
        return pl.pallas_call(
            make_kernel(side, nt, heads),
            name="star",
            out_shape=(vmem(span_q.shape, bf16), vmem((answer_rows, cols), bf16)),
            in_specs=[any_spec] * 7,
            out_specs=(vmem_spec, vmem_spec),
            scratch_shapes=[
                pltpu.SMEM(block_len.shape, jnp.int32),
                vmem((heads * new_rows, HD), bf16),
                vmem(span_kv.shape, bf16),
                vmem(cache_kv.shape, bf16),
                vmem(anchor_kv.shape, bf16),
                vmem(queries.shape, bf16),
                vmem(out_weight.shape, bf16),
                vmem((chunk, HD), f32),
                vmem((8, cache_kv.shape[1]), f32),
                vmem((chunk, HD), bf16),
                vmem((side, chunk, HD), bf16),
                vmem((side, side, chunk, HD), bf16),
                vmem((side, 2, side * own, HD), bf16),
                vmem((side, rows, HD), bf16),
                vmem((side, 1, rows), f32),
                vmem((side, rows, HD), bf16),
                vmem((side, 1, rows), f32),
                vmem((side, rows, HD), bf16),
                vmem((side, 1, rows), f32),
                vmem((rows, HD), bf16),
                vmem((side, rows, HD), bf16),
                vmem((side * rows, HD), f32),
                vmem((nt, answer_rows, cols), f32),
                vmem((nt, answer_rows, cols), f32),
                vmem((heads * new_rows, HD), f32),
                vmem((heads * new_rows, HD), f32),
                vmem((heads * new_rows, HD), f32),
                pltpu.SemaphoreType.DMA((6 + heads,)),
                pltpu.SemaphoreType.DMA((10, 8)),
                pltpu.SemaphoreType.DMA((10, 8)),
            ],
            compiler_params=pltpu.CompilerParams(collective_id=0, has_side_effects=True),
        )(block_len, span_q, span_kv, cache_kv, anchor_kv, queries, out_weight)

    return local


def solution(mesh):
    placed = (
        P("ctx", "tp"),
        P(None, "ctx", "tp"),
        P(None, "ctx", "tp"),
        P(None, "ctx", "tp"),
        P("ctx"),
        P("ctx", "tp"),
        P("tp", "ctx"),
    )
    return jax.shard_map(
        make_local(mesh.shape["ctx"], mesh.shape["tp"]),
        mesh=mesh,
        in_specs=placed,
        out_specs=(P("ctx", "tp"), P("tp", "ctx")),
        check_vma=False,
    )
```

```python
import math

import jax
import jax.numpy as jnp
from jax import lax
from jax.experimental import pallas as pl
from jax.experimental.pallas import tpu as pltpu
from jax.sharding import PartitionSpec as P

HD = 128
NEG = -1e30
MESH = pl.DeviceIdType.MESH
LOG2 = math.log2(math.e) / math.sqrt(HD)

SENDS = QA, QB, AB, AA, RO, RL, CO, CL, GB, TP = range(10)


def scores(q, k):
    return lax.dot_general(q, k, (((1,), (1,)), ((), ())), preferred_element_type=jnp.float32)


def softmax_parts(parts, values):
    peak = None
    for s in parts:
        top = jnp.max(s, axis=1, keepdims=True)
        peak = top if peak is None else jnp.maximum(peak, top)
    total, out = None, None
    for s, v in zip(parts, values):
        w = jnp.exp2((s - peak) * LOG2)
        part = jnp.sum(w, axis=1, keepdims=True)
        prod = jnp.dot(w.astype(jnp.bfloat16), v, preferred_element_type=jnp.float32)
        total = part if total is None else total + part
        out = prod if out is None else out + prod
    return peak, total, out


def wide(x, columns):
    return x if columns == x.shape[1] else jnp.concatenate([x] * (columns // x.shape[1]), axis=1)


def lane_softmax(parts, values, before=None):
    top = None
    for s in parts:
        for c in range(0, s.shape[1], HD):
            piece = s[:, c : c + HD]
            top = piece if top is None else jnp.maximum(top, piece)
    peak = jnp.broadcast_to(jnp.max(top, axis=1, keepdims=True), top.shape)
    if before is not None:
        peak = jnp.maximum(peak, before)
    total, out = None, None
    for s, v in zip(parts, values):
        w = jnp.exp2((s - wide(peak, s.shape[1])) * LOG2)
        for c in range(0, w.shape[1], HD):
            piece = w[:, c : c + HD]
            total = piece if total is None else total + piece
        prod = jnp.dot(w.astype(jnp.bfloat16), v, preferred_element_type=jnp.float32)
        out = prod if out is None else out + prod
    return peak, total, out


def make_kernel(side, nt, heads):
    ctx_count = side * side
    half = side // 2

    def kernel(
        len_hbm, span_q_hbm, span_kv_hbm, cache_hbm, anchor_hbm, queries_hbm, weight_hbm,
        out_any, ans_any,
        len_ref, span_q, span_kv, cache, anchor, queries, weight, q_rows, bias,
        mine, qx, q_all, anc, ro_send, rl_send, ro, rl, co, cl, done, att, att_f, proj, tpr,
        f_peak, f_sum, f_out, out, ans,
        in_sem, ss, rs, out_sem,
    ):
        rows = q_all.shape[1] * q_all.shape[2]
        ctx = lax.axis_index("ctx")
        t = lax.axis_index("tp")
        par = lax.rem(t, 2)
        lo, hi = lax.rem(ctx, side), lax.div(ctx, side)
        a = lo + par * (hi - lo)
        b = hi + par * (lo - hi)

        other = t + 1 - 2 * par

        def at(pa, pb, core):
            first = pb * side + pa
            return {"ctx": first + par * (pa * side + pb - first), "tp": core}

        def on_a(k):
            return at(lax.rem(a + k, side), b, t)

        def on_b(k):
            return at(a, lax.rem(b + k, side), t)

        def over_a(k):
            return at(lax.rem(a + k, side), b, other)

        def over_b(k):
            return at(a, lax.rem(b + k, side), other)

        def back(x, k):
            return lax.rem(x + side - k, side)

        def on_t(k):
            return {"tp": lax.rem(t + k, nt)}

        single = (QA, QB, AA)
        first_recv, used = {}, 0
        for x in SENDS:
            first_recv[x] = used
            used += side if x in single else 1

        def rcopy(src, dst, x, k, dev):
            return pltpu.make_async_remote_copy(
                src_ref=src, dst_ref=dst, send_sem=ss.at[x], recv_sem=rs.at[first_recv[x] + (k if x in single else 0)],
                device_id=dev, device_id_type=MESH,
            )

        new_rows = out.shape[0]
        pairs = [
            (queries_hbm, queries), (anchor_hbm, anchor), (len_hbm, len_ref), (cache_hbm, cache),
            (span_kv_hbm, span_kv), (weight_hbm, weight),
        ]
        for h in range(heads):
            pairs.append(
                (span_q_hbm.at[:, h * HD : (h + 1) * HD], span_q.at[h * new_rows : (h + 1) * new_rows])
            )
        loads = [
            pltpu.make_async_copy(src, dst, in_sem.at[min(i, 6)]) for i, (src, dst) in enumerate(pairs)
        ]
        barrier = pltpu.get_barrier_semaphore()
        for k in range(1, side):
            for peer in (on_a(k), on_b(k), over_a(k), over_b(k)):
                pl.semaphore_signal(barrier, inc=1, device_id=peer, device_id_type=MESH)
        for k in range(1, nt):
            pl.semaphore_signal(barrier, inc=1, device_id=on_t(k), device_id_type=MESH)

        for load in loads:
            load.start()

        loads[0].wait()
        loads[1].wait()
        wide = queries[...].astype(jnp.float32)
        for i in range(queries.shape[0]):
            for h in range(heads):
                q_rows[i * heads + h : i * heads + h + 1, :] = wide[i : i + 1, h * HD : (h + 1) * HD]
        mine[...] = q_rows[...].astype(jnp.bfloat16)
        own_rows = anchor.shape[1]
        anc[b, :, pl.ds(a * own_rows, own_rows), :] = anchor[...]
        loads[2].wait()
        length = len_ref[0]
        column = lax.broadcasted_iota(jnp.int32, bias.shape, 1)
        bias[...] = jnp.where(column < length, 0.0, NEG)

        pl.semaphore_wait(barrier, 4 * (side - 1) + nt - 1)

        far_first = sorted(range(1, side), key=lambda k: -min(k, side - k))
        far_all = far_first + [0]

        def qa(k, owner):
            return rcopy(mine, qx.at[owner], QA, k, over_a(k))

        def qb_chunk(k, chunk):
            return rcopy(qx.at[chunk], q_all.at[a, chunk], QB, k, over_a(k))

        def qb(k, owner):
            return rcopy(qx, q_all.at[owner], QB, k, over_a(k))

        def all_of(x, ref):
            return rcopy(ref, ref, x, 0, over_a(0))

        def ab(k, owner):
            place = anc.at[b, :, pl.ds(owner * own_rows, own_rows), :]
            return rcopy(place, place, AB, k, on_a(k))

        def right(step, slot):
            return rcopy(anc.at[slot], anc.at[slot], AA, step - 1, on_b(1))

        def left(step, slot):
            return rcopy(anc.at[slot], anc.at[slot], AA, half + step - 1, on_b(side - 1))

        def slot_at(offset):
            return lax.rem(b + side + offset, side)

        def ring_send(step):
            if step <= half:
                right(step, slot_at(1 - step)).start()
            if step <= half - 1:
                left(step, slot_at(step - 1)).start()

        def ring_recv(step):
            got = []
            if step <= half:
                got.append(slot_at(-step))
                right(step, got[-1]).wait_recv()
            if step <= half - 1:
                got.append(slot_at(step))
                left(step, got[-1]).wait_recv()
            return got

        for k in far_all:
            qa(k, a).start()

        group = min(heads, 4) * new_rows
        tri_row = lax.rem(lax.broadcasted_iota(jnp.int32, (group, new_rows), 0), new_rows)
        tri_col = lax.broadcasted_iota(jnp.int32, (group, new_rows), 1)

        def first_local(i, carry):
            r = pl.ds(pl.multiple_of(i * group, group), group)
            q = span_q[r, :]
            parts = [
                scores(q, cache[0]) + bias[0:1, :],
                jnp.where(tri_col <= tri_row, scores(q, span_kv[0]), NEG),
            ]
            peak, total, o = lane_softmax(parts, [cache[1], span_kv[1]])
            f_peak[r, :] = peak
            f_sum[r, :] = total
            f_out[r, :] = o
            return carry

        def first_anchor(slots, last=False):
            def body(i, carry):
                r = pl.ds(pl.multiple_of(i * group, group), group)
                q = span_q[r, :]
                parts = [scores(q, anc[s, 0]) for s in slots]
                before = f_peak[r, :]
                peak, total, o = lane_softmax(parts, [anc[s, 1] for s in slots], before)
                shrink = jnp.exp2((before - peak) * LOG2)
                total = f_sum[r, :] * shrink + total
                o = f_out[r, :] * shrink + o
                if last:
                    f_out[r, :] = o / jnp.sum(total, axis=1, keepdims=True)
                else:
                    f_peak[r, :] = peak
                    f_sum[r, :] = total
                    f_out[r, :] = o
                return carry

            lax.fori_loop(0, heads * new_rows // group, body, 0)

        for load in loads[3:6]:
            load.wait()
        pltpu.make_async_copy(span_q, span_q, in_sem.at[6]).wait()
        def forward(offsets):
            for d in offsets:
                chunk = back(b, d)
                qa(d, chunk).wait_recv()
                for k in far_all:
                    qb_chunk(k, chunk).start()

        groups = heads * new_rows // group
        lax.fori_loop(0, (groups + 1) // 2, first_local, 0)
        for k in far_first:
            ab(k, a).start()
        forward([0] + sorted({1, side - 1}))
        for d in range(2, half + 1):
            forward(sorted({d, side - d}))
        diag = lax.broadcasted_iota(jnp.int32, (rows, rows), 0) == lax.broadcasted_iota(
            jnp.int32, (rows, rows), 1
        )

        def as_row(col):
            return jnp.sum(jnp.where(diag, col, 0.0), axis=0, keepdims=True)

        def as_col(row):
            return jnp.sum(jnp.where(diag, row, 0.0), axis=1, keepdims=True)

        def query_blocks(owners):
            q = [q_all[owner].reshape(rows, HD) for owner in owners]
            q = q[0] if len(q) == 1 else jnp.concatenate(q, axis=0)
            parts = [
                scores(q, cache[0]) + bias[0:1, :],
                scores(q, span_kv[0]),
                scores(q, anchor[0]),
            ]
            peak, total, o = softmax_parts(parts, [cache[1], span_kv[1], anchor[1]])
            o = (o / total).astype(jnp.bfloat16)
            lse = peak * LOG2 + jnp.log2(total)
            for i, owner in enumerate(owners):
                ro_send[owner] = o[i * rows : (i + 1) * rows]
                rl_send[owner] = as_row(lse[i * rows : (i + 1) * rows])

        def ro_copy(k, block, owner):
            return rcopy(ro_send.at[block], ro.at[owner], RO, k, over_b(k))

        def rl_copy(k, block, owner):
            return rcopy(rl_send.at[block], rl.at[owner], RL, k, over_b(k))

        def some_blocks(offsets):
            owners = [back(b, k) for k in offsets]
            for k, owner in zip(offsets, owners):
                qb(k, owner).wait_recv()
            query_blocks(owners)
            for k, owner in zip(offsets, owners):
                k = lax.rem(side - k, side)
                ro_copy(k, owner, b).start()
                rl_copy(k, owner, b).start()

        some_blocks([0])

        all_of(AB, anc.at[b, :, pl.ds(0, (side - 1) * own_rows), :]).wait_recv()
        ring_send(1)


        def two_blocks(i, carry):
            some_blocks([i, side - i])
            return carry

        lax.fori_loop(1, half, two_blocks, 0)
        some_blocks([half])

        lax.fori_loop((groups + 1) // 2, groups, first_local, 0)
        slots = [b] + ring_recv(1)
        ring_send(2)

        def combine(o_ref, l_ref):
            lse = [l_ref[i] for i in range(side)]
            peak = lse[0]
            for x in lse[1:]:
                peak = jnp.maximum(peak, x)
            weights = [jnp.exp2(x - peak) for x in lse]
            total = weights[0]
            for w in weights[1:]:
                total = total + w
            o = None
            for i in range(side):
                term = as_col(weights[i] / total) * o_ref[i].astype(jnp.float32)
                o = term if o is None else o + term
            return o.astype(jnp.bfloat16), peak + jnp.log2(total)

        all_of(RO, ro).wait_recv()
        all_of(RL, rl).wait_recv()
        o, lse = combine(ro, rl)
        co[b] = o
        cl[b] = lse

        def co_copy(k, owner):
            return rcopy(co.at[owner], co.at[owner], CO, k, on_b(k))

        def cl_copy(k, owner):
            return rcopy(cl.at[owner], cl.at[owner], CL, k, on_b(k))

        for k in far_first:
            co_copy(k, b).start()
            cl_copy(k, b).start()

        if half > 1:
            slots = slots + ring_recv(2)
        first_anchor(slots, last=half <= 2)
        ring_send(3)

        all_of(CO, co.at[0 : side - 1]).wait_recv()
        all_of(CL, cl.at[0 : side - 1]).wait_recv()
        o, _ = combine(co, cl)
        done[...] = o

        def gb(k, owner):
            return rcopy(done, att.at[owner], GB, k, over_a(k))

        for k in far_all:
            gb(k, a).start()

        for step in range(3, half):
            slots = ring_recv(step)
            first_anchor(slots)
            ring_send(step + 1)

        all_of(GB, att).wait_recv()
        att_f[...] = att[...].reshape(-1, HD).astype(jnp.float32)
        count = att_f.shape[0] // heads
        per = count // ctx_count
        row = lax.broadcasted_iota(jnp.int32, (count, count), 0)
        col = lax.broadcasted_iota(jnp.int32, (count, count), 1)
        dev, sub = lax.div(row, per), lax.rem(row, per)
        swapped = (lax.rem(dev, side) * side + lax.div(dev, side)) * per + sub
        source = row + par * (swapped - row)
        perm = jnp.where(col == source, 1.0, 0.0).astype(jnp.bfloat16)
        total = None
        for h in range(heads):
            rows_h = att_f[pl.ds(h, count, stride=heads), :].astype(jnp.bfloat16)
            rows_h = jnp.dot(perm, rows_h, preferred_element_type=jnp.float32)
            term = jnp.dot(
                rows_h.astype(jnp.bfloat16), weight[h * HD : (h + 1) * HD, :],
                preferred_element_type=jnp.float32,
            )
            total = term if total is None else total + term
        proj[...] = total.reshape(proj.shape)
        tpr[t] = proj[t]

        def tp_copy(k, piece, owner):
            return rcopy(proj.at[piece], tpr.at[owner], TP, k, on_t(k))

        for k in range(1, nt):
            tp_copy(k, lax.rem(t + k, nt), t).start()

        if half > 2:
            slots = ring_recv(half)
            first_anchor(slots, last=True)
        for h in range(heads):
            out[:, h * HD : (h + 1) * HD] = f_out[h * new_rows : (h + 1) * new_rows, :].astype(jnp.bfloat16)
        store = pltpu.make_async_copy(out, out_any, out_sem.at[0])
        store.start()

        all_of(TP, tpr.at[0 : nt - 1]).wait_recv()
        total = tpr[0]
        for i in range(1, nt):
            total = total + tpr[i]
        ans[...] = total.astype(jnp.bfloat16)
        final = pltpu.make_async_copy(ans, ans_any, out_sem.at[1])
        final.start()

        for x, ref in (
            (QA, qx), (QB, q_all), (AB, anc.at[b, :, pl.ds(0, (side - 1) * own_rows), :]),
            (AA, anc.at[0 : side - 1]), (RO, ro), (RL, rl), (CO, co.at[0 : side - 1]),
            (CL, cl.at[0 : side - 1]), (GB, att), (TP, tpr.at[0 : nt - 1]),
        ):
            all_of(x, ref).wait_send()
        store.wait()
        final.wait()

    return kernel


def make_local(ctx_count, nt):
    side = math.isqrt(ctx_count)

    def local(span_q, span_kv, cache_kv, anchor_kv, block_len, queries, out_weight):
        new_rows = span_q.shape[0]
        heads = span_q.shape[1] // HD
        per = queries.shape[0]
        chunk = per * heads
        rows = side * chunk
        own = anchor_kv.shape[1]
        cols = out_weight.shape[1]
        answer_rows = per * ctx_count // nt
        any_spec = pl.BlockSpec(memory_space=pl.ANY)
        bf16, f32 = jnp.bfloat16, jnp.float32
        vmem = pltpu.VMEM
        return pl.pallas_call(
            make_kernel(side, nt, heads),
            name="star",
            out_shape=(vmem(span_q.shape, bf16), vmem((answer_rows, cols), bf16)),
            in_specs=[pl.BlockSpec(memory_space=pltpu.HBM)] + [any_spec] * 6,
            out_specs=(any_spec, any_spec),
            scratch_shapes=[
                pltpu.SMEM(block_len.shape, jnp.int32),
                vmem((heads * new_rows, HD), bf16),
                vmem(span_kv.shape, bf16),
                vmem(cache_kv.shape, bf16),
                vmem(anchor_kv.shape, bf16),
                vmem(queries.shape, bf16),
                vmem(out_weight.shape, bf16),
                vmem((chunk, HD), f32),
                vmem((8, cache_kv.shape[1]), f32),
                vmem((chunk, HD), bf16),
                vmem((side, chunk, HD), bf16),
                vmem((side, side, chunk, HD), bf16),
                vmem((side, 2, side * own, HD), bf16),
                vmem((side, rows, HD), bf16),
                vmem((side, 1, rows), f32),
                vmem((side, rows, HD), bf16),
                vmem((side, 1, rows), f32),
                vmem((side, rows, HD), bf16),
                vmem((side, 1, rows), f32),
                vmem((rows, HD), bf16),
                vmem((side, rows, HD), bf16),
                vmem((side * rows, HD), f32),
                vmem((nt, answer_rows, cols), f32),
                vmem((nt, answer_rows, cols), f32),
                vmem((heads * new_rows, HD), f32),
                vmem((heads * new_rows, HD), f32),
                vmem((heads * new_rows, HD), f32),
                vmem(span_q.shape, bf16),
                vmem((answer_rows, cols), bf16),
                pltpu.SemaphoreType.DMA((7,)),
                pltpu.SemaphoreType.DMA((len(SENDS),)),
                pltpu.SemaphoreType.DMA((len(SENDS) + 3 * (side - 1),)),
                pltpu.SemaphoreType.DMA((2,)),
            ],
            compiler_params=pltpu.CompilerParams(collective_id=0, has_side_effects=True),
        )(block_len, span_q, span_kv, cache_kv, anchor_kv, queries, out_weight)

    return local


def solution(mesh):
    placed = (
        P("ctx", "tp"),
        P(None, "ctx", "tp"),
        P(None, "ctx", "tp"),
        P(None, "ctx", "tp"),
        P("ctx"),
        P("ctx", "tp"),
        P("tp", "ctx"),
    )
    return jax.shard_map(
        make_local(mesh.shape["ctx"], mesh.shape["tp"]),
        mesh=mesh,
        in_specs=placed,
        out_specs=(P("ctx", "tp"), P("tp", "ctx")),
        check_vma=False,
    )
```

```python
import math

import jax
import jax.numpy as jnp
from jax import lax
from jax.experimental import pallas as pl
from jax.experimental.pallas import tpu as pltpu
from jax.sharding import PartitionSpec as P

HD = 128
NEG = -1e30
MESH = pl.DeviceIdType.MESH
LOG2 = math.log2(math.e) / math.sqrt(HD)

SENDS = QA, QB, AB, AA, RO, RL, CO, CL, GB, TP = range(10)


def scores(q, k):
    return lax.dot_general(q, k, (((1,), (1,)), ((), ())), preferred_element_type=jnp.float32)


def softmax_parts(parts, values):
    peak = None
    for s in parts:
        top = jnp.max(s, axis=1, keepdims=True)
        peak = top if peak is None else jnp.maximum(peak, top)
    total, out = None, None
    for s, v in zip(parts, values):
        w = jnp.exp2((s - peak) * LOG2)
        part = jnp.sum(w, axis=1, keepdims=True)
        prod = jnp.dot(w.astype(jnp.bfloat16), v, preferred_element_type=jnp.float32)
        total = part if total is None else total + part
        out = prod if out is None else out + prod
    return peak, total, out


def wide(x, columns):
    return x if columns == x.shape[1] else jnp.concatenate([x] * (columns // x.shape[1]), axis=1)


def lane_softmax(parts, values, before=None):
    top = None
    for s in parts:
        for c in range(0, s.shape[1], HD):
            piece = s[:, c : c + HD]
            top = piece if top is None else jnp.maximum(top, piece)
    peak = jnp.broadcast_to(jnp.max(top, axis=1, keepdims=True), top.shape)
    if before is not None:
        peak = jnp.maximum(peak, before)
    total, out = None, None
    for s, v in zip(parts, values):
        w = jnp.exp2((s - wide(peak, s.shape[1])) * LOG2)
        for c in range(0, w.shape[1], HD):
            piece = w[:, c : c + HD]
            total = piece if total is None else total + piece
        prod = jnp.dot(w.astype(jnp.bfloat16), v, preferred_element_type=jnp.float32)
        out = prod if out is None else out + prod
    return peak, total, out


def make_kernel(side, nt, heads):
    ctx_count = side * side
    half = side // 2

    def kernel(
        len_hbm, span_q_hbm, span_kv_hbm, cache_hbm, anchor_hbm, queries_hbm, weight_hbm,
        out_any, ans_any,
        len_ref, span_q, span_kv, cache, anchor, queries, weight, q_rows, bias,
        mine, qx, q_all, anc, ro_send, rl_send, ro, rl, co, cl, done, att, att_f, proj, tpr,
        f_peak, f_sum, f_out, out, ans,
        in_sem, ss, rs, out_sem,
    ):
        rows = q_all.shape[1] * q_all.shape[2]
        ctx = lax.axis_index("ctx")
        t = lax.axis_index("tp")
        par = lax.rem(t, 2)
        lo, hi = lax.rem(ctx, side), lax.div(ctx, side)
        a = lo + par * (hi - lo)
        b = hi + par * (lo - hi)

        other = t + 1 - 2 * par
        core_one = t + 1 - par

        def at(pa, pb, core):
            first = pb * side + pa
            return {"ctx": first + par * (pa * side + pb - first), "tp": core}

        def on_a(k):
            return at(lax.rem(a + k, side), b, t)

        def on_b(k):
            return at(a, lax.rem(b + k, side), t)

        def over_a(k):
            return at(lax.rem(a + k, side), b, other)

        def over_b(k):
            return at(a, lax.rem(b + k, side), other)

        def to_one(k):
            return at(a, lax.rem(b + k, side), core_one)

        def back(x, k):
            return lax.rem(x + side - k, side)

        def on_t(k):
            return {"tp": lax.rem(t + k, nt)}

        single = (QA, QB, AA)
        first_recv, used = {}, 0
        for x in SENDS:
            first_recv[x] = used
            used += side if x in single else 2

        second = {CO: len(SENDS), CL: len(SENDS) + 1, GB: len(SENDS) + 2}

        def rcopy(src, dst, x, k, dev, d=0):
            return pltpu.make_async_remote_copy(
                src_ref=src, dst_ref=dst, send_sem=ss.at[second[x] if d else x], recv_sem=rs.at[first_recv[x] + k],
                device_id=dev, device_id_type=MESH,
            )

        new_rows = out.shape[0]
        pairs = [
            (queries_hbm, queries), (anchor_hbm, anchor), (len_hbm, len_ref), (cache_hbm, cache),
            (span_kv_hbm, span_kv), (weight_hbm, weight),
        ]
        for h in range(heads):
            pairs.append(
                (span_q_hbm.at[:, h * HD : (h + 1) * HD], span_q.at[h * new_rows : (h + 1) * new_rows])
            )
        loads = [
            pltpu.make_async_copy(src, dst, in_sem.at[min(i, 6)]) for i, (src, dst) in enumerate(pairs)
        ]
        barrier = pltpu.get_barrier_semaphore()
        for k in range(1, side):
            for peer in (on_a(k), on_b(k), over_a(k), over_b(k)):
                pl.semaphore_signal(barrier, inc=1, device_id=peer, device_id_type=MESH)
        for k in range(1, nt):
            pl.semaphore_signal(barrier, inc=1, device_id=on_t(k), device_id_type=MESH)

        for load in loads:
            load.start()

        loads[0].wait()
        loads[1].wait()
        wide = queries[...].astype(jnp.float32)
        for i in range(queries.shape[0]):
            for h in range(heads):
                q_rows[i * heads + h : i * heads + h + 1, :] = wide[i : i + 1, h * HD : (h + 1) * HD]
        mine[...] = q_rows[...].astype(jnp.bfloat16)
        own_rows = anchor.shape[1]
        anc[b, :, pl.ds(a * own_rows, own_rows), :] = anchor[...]
        loads[2].wait()
        length = len_ref[0]
        column = lax.broadcasted_iota(jnp.int32, bias.shape, 1)
        bias[...] = jnp.where(column < length, 0.0, NEG)

        pl.semaphore_wait(barrier, 4 * (side - 1) + nt - 1)

        far_first = sorted(range(1, side), key=lambda k: -min(k, side - k))
        far_all = far_first + [0]

        def qa(k, owner):
            return rcopy(mine, qx.at[owner], QA, k, over_a(k))

        def qb_chunk(k, chunk):
            return rcopy(qx.at[chunk], q_all.at[a, chunk], QB, k, over_a(k))

        def qb(k, owner):
            return rcopy(qx, q_all.at[owner], QB, k, over_a(k))

        def all_of(x, ref, k=0, d=0):
            return rcopy(ref, ref, x, k, over_a(0), d)

        def ab(k, owner):
            place = anc.at[b, :, pl.ds(owner * own_rows, own_rows), :]
            return rcopy(place, place, AB, 0, on_a(k))

        def right(step, slot):
            place = anc.at[slot] if step < half else anc.at[slot, 0]
            return rcopy(place, place, AA, step - 1, on_b(1))

        def left(step, slot):
            place = anc.at[slot] if step < half else anc.at[slot, 1]
            return rcopy(place, place, AA, half + step - 1, on_b(side - 1))

        def slot_at(offset):
            return lax.rem(b + side + offset, side)

        def ring_send(step):
            if step <= half:
                right(step, slot_at(1 - step)).start()
                left(step, slot_at(step - 1)).start()

        def ring_send_on(core, step):
            @pl.when(par == core)
            def _():
                ring_send(step)

        def ring_recv(step):
            got = [slot_at(-step), slot_at(step)]
            right(step, got[0]).wait_recv()
            left(step, got[1]).wait_recv()
            if step == half:
                got = got[:1]
            return got

        for k in far_all:
            qa(k, a).start()

        group = min(heads, 4) * new_rows
        tri_row = lax.rem(lax.broadcasted_iota(jnp.int32, (group, new_rows), 0), new_rows)
        tri_col = lax.broadcasted_iota(jnp.int32, (group, new_rows), 1)

        def first_local(i, carry):
            r = pl.ds(pl.multiple_of(i * group, group), group)
            q = span_q[r, :]
            parts = [
                scores(q, cache[0]) + bias[0:1, :],
                jnp.where(tri_col <= tri_row, scores(q, span_kv[0]), NEG),
            ]
            peak, total, o = lane_softmax(parts, [cache[1], span_kv[1]])
            f_peak[r, :] = peak
            f_sum[r, :] = total
            f_out[r, :] = o
            return carry

        def first_anchor(slots, last=False):
            def body(i, carry):
                r = pl.ds(pl.multiple_of(i * group, group), group)
                q = span_q[r, :]
                parts = [scores(q, anc[s, 0]) for s in slots]
                before = f_peak[r, :]
                peak, total, o = lane_softmax(parts, [anc[s, 1] for s in slots], before)
                shrink = jnp.exp2((before - peak) * LOG2)
                total = f_sum[r, :] * shrink + total
                o = f_out[r, :] * shrink + o
                if last:
                    f_out[r, :] = o / jnp.sum(total, axis=1, keepdims=True)
                else:
                    f_peak[r, :] = peak
                    f_sum[r, :] = total
                    f_out[r, :] = o
                return carry

            lax.fori_loop(0, heads * new_rows // group, body, 0)

        for load in loads[3:6]:
            load.wait()
        pltpu.make_async_copy(span_q, span_q, in_sem.at[6]).wait()
        def forward(offsets):
            for d in offsets:
                chunk = back(b, d)
                qa(d, chunk).wait_recv()
                for k in far_all:
                    qb_chunk(k, chunk).start()

        groups = heads * new_rows // group
        lax.fori_loop(0, (groups + 1) // 2, first_local, 0)
        for k in far_first:
            ab(k, a).start()
        forward([0] + sorted({1, side - 1}))
        for d in range(2, half + 1):
            forward(sorted({d, side - d}))
        diag = lax.broadcasted_iota(jnp.int32, (rows, rows), 0) == lax.broadcasted_iota(
            jnp.int32, (rows, rows), 1
        )

        def as_row(col):
            return jnp.sum(jnp.where(diag, col, 0.0), axis=0, keepdims=True)

        def as_col(row):
            return jnp.sum(jnp.where(diag, row, 0.0), axis=1, keepdims=True)

        def query_blocks(owners):
            q = [q_all[owner].reshape(rows, HD) for owner in owners]
            q = q[0] if len(q) == 1 else jnp.concatenate(q, axis=0)
            parts = [
                scores(q, cache[0]) + bias[0:1, :],
                scores(q, span_kv[0]),
                scores(q, anchor[0]),
            ]
            peak, total, o = softmax_parts(parts, [cache[1], span_kv[1], anchor[1]])
            o = (o / total).astype(jnp.bfloat16)
            lse = peak * LOG2 + jnp.log2(total)
            for i, owner in enumerate(owners):
                ro_send[owner] = o[i * rows : (i + 1) * rows]
                rl_send[owner] = as_row(lse[i * rows : (i + 1) * rows])

        def ro_copy(k, block):
            return rcopy(ro_send.at[block], ro.at[par, b], RO, par, to_one(k))

        def rl_copy(k, block):
            return rcopy(rl_send.at[block], rl.at[par, b], RL, par, to_one(k))

        def some_blocks(offsets):
            owners = [back(b, k) for k in offsets]
            for k, owner in zip(offsets, owners):
                qb(k, owner).wait_recv()
            query_blocks(owners)
            for k, owner in zip(offsets, owners):
                if isinstance(k, int) and k == 0:

                    @pl.when(par == 1)
                    def _():
                        ro[1, b] = ro_send[b]
                        rl[1, b] = rl_send[b]

                    @pl.when(par == 0)
                    def _():
                        ro_copy(0, b).start()
                        rl_copy(0, b).start()

                else:
                    ro_copy(side - k, owner).start()
                    rl_copy(side - k, owner).start()

        some_blocks([0])

        all_of(AB, anc.at[b, :, pl.ds(0, (side - 1) * own_rows), :]).wait_recv()
        ring_send(1)


        def two_blocks(i, carry):
            some_blocks([half - i, half + i])
            return carry

        if half > 1:
            some_blocks([1, side - 1])
        some_blocks([half])
        lax.fori_loop(1, half - 1, two_blocks, 0)

        slots = [b] + ring_recv(1)
        ring_send_on(0, 2)
        lax.fori_loop((groups + 1) // 2, groups, first_local, 0)
        ring_send_on(1, 2)

        def combine(o_ref, l_ref, d):
            lse = [l_ref[d, i] for i in range(side)]
            peak = lse[0]
            for x in lse[1:]:
                peak = jnp.maximum(peak, x)
            weights = [jnp.exp2(x - peak) for x in lse]
            total = weights[0]
            for w in weights[1:]:
                total = total + w
            o = None
            for i in range(side):
                term = as_col(weights[i] / total) * o_ref[d, i].astype(jnp.float32)
                o = term if o is None else o + term
            return o.astype(jnp.bfloat16), peak + jnp.log2(total)

        def plane_slot(d):
            return a if d else b

        def plane_peer(d, k):
            return on_a(k) if d else on_b(k)

        def co_copy(d, k):
            place = co.at[d, plane_slot(d)]
            return rcopy(place, place, CO, d, plane_peer(d, k), d)

        def cl_copy(d, k):
            place = cl.at[d, plane_slot(d)]
            return rcopy(place, place, CL, d, plane_peer(d, k), d)

        def blocks_of(d):
            return slice(0, side - 1) if d else slice(0, side)


        @pl.when(par == 1)
        def _():
            for d in (1, 0):
                all_of(RO, ro.at[d, blocks_of(d)], d).wait_recv()
                all_of(RL, rl.at[d, blocks_of(d)], d).wait_recv()
                o, lse = combine(ro, rl, d)
                co[d, plane_slot(d)] = o
                cl[d, plane_slot(d)] = lse
                for k in far_first:
                    co_copy(d, k).start()
                    cl_copy(d, k).start()

        if half > 1:
            slots = slots + ring_recv(2)
        first_anchor(slots, last=half <= 2)
        ring_send(3)

        def gb(d, k):
            if d:
                return rcopy(done.at[1], att.at[b], GB, 0, on_b(k), d)
            return rcopy(done.at[0], att.at[a], GB, 0, over_a(k))


        @pl.when(par == 1)
        def _():
            for d in (1, 0):
                all_of(CO, co.at[d, 0 : side - 1], d).wait_recv()
                all_of(CL, cl.at[d, 0 : side - 1], d).wait_recv()
                o, _ = combine(co, cl, d)
                done[d] = o
                for k in far_first if d else far_all:
                    gb(d, k).start()
                if d:
                    att[b] = o

        for step in range(3, half):
            slots = ring_recv(step)
            first_anchor(slots)
            ring_send(step + 1)

        for d in (0, 1):

            @pl.when(par == d)
            def _():
                all_of(GB, att.at[blocks_of(d)]).wait_recv()

        att_f[...] = att[...].reshape(-1, HD).astype(jnp.float32)
        count = att_f.shape[0] // heads
        per = count // ctx_count
        row = lax.broadcasted_iota(jnp.int32, (count, count), 0)
        col = lax.broadcasted_iota(jnp.int32, (count, count), 1)
        dev, sub = lax.div(row, per), lax.rem(row, per)
        swapped = (lax.rem(dev, side) * side + lax.div(dev, side)) * per + sub
        source = row + par * (swapped - row)
        perm = jnp.where(col == source, 1.0, 0.0).astype(jnp.bfloat16)
        total = None
        for h in range(heads):
            rows_h = att_f[pl.ds(h, count, stride=heads), :].astype(jnp.bfloat16)
            rows_h = jnp.dot(perm, rows_h, preferred_element_type=jnp.float32)
            term = jnp.dot(
                rows_h.astype(jnp.bfloat16), weight[h * HD : (h + 1) * HD, :],
                preferred_element_type=jnp.float32,
            )
            total = term if total is None else total + term
        proj[...] = total.reshape(proj.shape)
        tpr[t] = proj[t]

        def tp_copy(k, piece, owner):
            return rcopy(proj.at[piece], tpr.at[owner], TP, 0, on_t(k))

        for k in range(1, nt):
            tp_copy(k, lax.rem(t + k, nt), t).start()

        if half > 2:
            slots = ring_recv(half)
            first_anchor(slots, last=True)
        for h in range(heads):
            out[:, h * HD : (h + 1) * HD] = f_out[h * new_rows : (h + 1) * new_rows, :].astype(jnp.bfloat16)
        store = pltpu.make_async_copy(out, out_any, out_sem.at[0])
        store.start()

        all_of(TP, tpr.at[0 : nt - 1]).wait_recv()
        total = tpr[0]
        for i in range(1, nt):
            total = total + tpr[i]
        ans[...] = total.astype(jnp.bfloat16)
        final = pltpu.make_async_copy(ans, ans_any, out_sem.at[1])
        final.start()

        for x, ref in (
            (QA, qx), (QB, q_all), (AB, anc.at[b, :, pl.ds(0, (side - 1) * own_rows), :]),
            (AA, anc.at[0 : side - 1]), (TP, tpr.at[0 : nt - 1]),
        ):
            all_of(x, ref).wait_send()
        for d in (0, 1):

            @pl.when(par == d)
            def _():
                all_of(RO, ro_send.at[blocks_of(d)]).wait_send()
                all_of(RL, rl_send.at[blocks_of(d)]).wait_send()

        @pl.when(par == 1)
        def _():
            for d in (0, 1):
                all_of(CO, co.at[d, 0 : side - 1], d, d).wait_send()
                all_of(CL, cl.at[d, 0 : side - 1], d, d).wait_send()
                all_of(GB, att.at[blocks_of(d)], 0, d).wait_send()

        store.wait()
        final.wait()

    return kernel


def make_local(ctx_count, nt):
    side = math.isqrt(ctx_count)

    def local(span_q, span_kv, cache_kv, anchor_kv, block_len, queries, out_weight):
        new_rows = span_q.shape[0]
        heads = span_q.shape[1] // HD
        per = queries.shape[0]
        chunk = per * heads
        rows = side * chunk
        own = anchor_kv.shape[1]
        cols = out_weight.shape[1]
        answer_rows = per * ctx_count // nt
        any_spec = pl.BlockSpec(memory_space=pl.ANY)
        bf16, f32 = jnp.bfloat16, jnp.float32
        vmem = pltpu.VMEM
        return pl.pallas_call(
            make_kernel(side, nt, heads),
            name="star",
            out_shape=(vmem(span_q.shape, bf16), vmem((answer_rows, cols), bf16)),
            in_specs=[pl.BlockSpec(memory_space=pltpu.HBM)] + [any_spec] * 6,
            out_specs=(any_spec, any_spec),
            scratch_shapes=[
                pltpu.SMEM(block_len.shape, jnp.int32),
                vmem((heads * new_rows, HD), bf16),
                vmem(span_kv.shape, bf16),
                vmem(cache_kv.shape, bf16),
                vmem(anchor_kv.shape, bf16),
                vmem(queries.shape, bf16),
                vmem(out_weight.shape, bf16),
                vmem((chunk, HD), f32),
                vmem((8, cache_kv.shape[1]), f32),
                vmem((chunk, HD), bf16),
                vmem((side, chunk, HD), bf16),
                vmem((side, side, chunk, HD), bf16),
                vmem((side, 2, side * own, HD), bf16),
                vmem((side, rows, HD), bf16),
                vmem((side, 1, rows), f32),
                vmem((2, side, rows, HD), bf16),
                vmem((2, side, 1, rows), f32),
                vmem((2, side, rows, HD), bf16),
                vmem((2, side, 1, rows), f32),
                vmem((2, rows, HD), bf16),
                vmem((side, rows, HD), bf16),
                vmem((side * rows, HD), f32),
                vmem((nt, answer_rows, cols), f32),
                vmem((nt, answer_rows, cols), f32),
                vmem((heads * new_rows, HD), f32),
                vmem((heads * new_rows, HD), f32),
                vmem((heads * new_rows, HD), f32),
                vmem(span_q.shape, bf16),
                vmem((answer_rows, cols), bf16),
                pltpu.SemaphoreType.DMA((7,)),
                pltpu.SemaphoreType.DMA((len(SENDS) + 3,)),
                pltpu.SemaphoreType.DMA((2 * len(SENDS) + 3 * (side - 2),)),
                pltpu.SemaphoreType.DMA((2,)),
            ],
            compiler_params=pltpu.CompilerParams(collective_id=0, has_side_effects=True),
        )(block_len, span_q, span_kv, cache_kv, anchor_kv, queries, out_weight)

    return local


def solution(mesh):
    placed = (
        P("ctx", "tp"),
        P(None, "ctx", "tp"),
        P(None, "ctx", "tp"),
        P(None, "ctx", "tp"),
        P("ctx"),
        P("ctx", "tp"),
        P("tp", "ctx"),
    )
    return jax.shard_map(
        make_local(mesh.shape["ctx"], mesh.shape["tp"]),
        mesh=mesh,
        in_specs=placed,
        out_specs=(P("ctx", "tp"), P("tp", "ctx")),
        check_vma=False,
    )
```

```python
import math

import jax
import jax.numpy as jnp
from jax import lax
from jax.experimental import pallas as pl
from jax.experimental.pallas import tpu as pltpu
from jax.sharding import PartitionSpec as P

HD = 128
NEG = -1e30
MESH = pl.DeviceIdType.MESH
LOG2 = math.log2(math.e) / math.sqrt(HD)

SENDS = QA, QB, AB, AA, RO, RL, CO, CL, GB, TP = range(10)


def scores(q, k):
    return lax.dot_general(q, k, (((1,), (1,)), ((), ())), preferred_element_type=jnp.float32)


def wide(x, columns):
    return x if columns == x.shape[1] else jnp.concatenate([x] * (columns // x.shape[1]), axis=1)


def lane_softmax(parts, values, before=None):
    top = None
    for s in parts:
        for c in range(0, s.shape[1], HD):
            piece = s[:, c : c + HD]
            top = piece if top is None else jnp.maximum(top, piece)
    peak = jnp.broadcast_to(jnp.max(top, axis=1, keepdims=True), top.shape)
    if before is not None:
        peak = jnp.maximum(peak, before)
    total, out = None, None
    for s, v in zip(parts, values):
        w = jnp.exp2((s - wide(peak, s.shape[1])) * LOG2)
        for c in range(0, w.shape[1], HD):
            piece = w[:, c : c + HD]
            total = piece if total is None else total + piece
        prod = jnp.dot(w.astype(jnp.bfloat16), v, preferred_element_type=jnp.float32)
        out = prod if out is None else out + prod
    return peak, total, out


def make_kernel(side, nt, heads):
    ctx_count = side * side
    half = side // 2

    def kernel(
        len_hbm, span_q_hbm, span_kv_hbm, cache_hbm, anchor_hbm, queries_hbm, weight_hbm,
        out_any, ans_any,
        len_ref, span_q, kv, queries, weight, q_rows, bias, bias_col, values,
        mine, qx, q_all, anc, ro_send, rl_send, ro, rl, co, cl, done, att, att_f, proj, tpr,
        f_peak, f_sum, f_out, out, ans,
        in_sem, ss, rs, out_sem,
    ):
        rows = q_all.shape[1] * q_all.shape[2]
        ctx = lax.axis_index("ctx")
        t = lax.axis_index("tp")
        par = lax.rem(t, 2)
        lo, hi = lax.rem(ctx, side), lax.div(ctx, side)
        a = lo + par * (hi - lo)
        b = hi + par * (lo - hi)

        other = t + 1 - 2 * par
        core_one = t + 1 - par

        def at(pa, pb, core):
            first = pb * side + pa
            return {"ctx": first + par * (pa * side + pb - first), "tp": core}

        def on_a(k):
            return at(lax.rem(a + k, side), b, t)

        def on_b(k):
            return at(a, lax.rem(b + k, side), t)

        def over_a(k):
            return at(lax.rem(a + k, side), b, other)

        def over_b(k):
            return at(a, lax.rem(b + k, side), other)

        def to_one(k):
            return at(a, lax.rem(b + k, side), core_one)

        def back(x, k):
            return lax.rem(x + side - k, side)

        def on_t(k):
            return {"tp": lax.rem(t + k, nt)}

        single = (QA, QB, AA)
        first_recv, used = {}, 0
        for x in SENDS:
            first_recv[x] = used
            used += side if x in single else 2

        second = {CO: len(SENDS), CL: len(SENDS) + 1, GB: len(SENDS) + 2}

        def rcopy(src, dst, x, k, dev, d=0):
            return pltpu.make_async_remote_copy(
                src_ref=src, dst_ref=dst, send_sem=ss.at[second[x] if d else x], recv_sem=rs.at[first_recv[x] + k],
                device_id=dev, device_id_type=MESH,
            )

        new_rows = out.shape[0]
        own_rows = anchor_hbm.shape[1]
        cached = cache_hbm.shape[1]
        near = cached + new_rows
        used = near + own_rows
        pairs = [
            (queries_hbm, queries), (anchor_hbm, kv.at[:, near:used]), (len_hbm, len_ref),
            (cache_hbm, kv.at[:, 0:cached]), (span_kv_hbm, kv.at[:, cached:near]), (weight_hbm, weight),
        ]
        for h in range(heads):
            pairs.append(
                (span_q_hbm.at[:, h * HD : (h + 1) * HD], span_q.at[h * new_rows : (h + 1) * new_rows])
            )
        loads = [
            pltpu.make_async_copy(src, dst, in_sem.at[min(i, 6)]) for i, (src, dst) in enumerate(pairs)
        ]
        barrier = pltpu.get_barrier_semaphore()
        for k in range(1, side):
            for peer in (on_a(k), on_b(k), over_a(k), over_b(k)):
                pl.semaphore_signal(barrier, inc=1, device_id=peer, device_id_type=MESH)
        for k in range(1, nt):
            pl.semaphore_signal(barrier, inc=1, device_id=on_t(k), device_id_type=MESH)

        for load in loads:
            load.start()

        loads[0].wait()
        loads[1].wait()
        flat = queries[...].astype(jnp.float32)
        for i in range(queries.shape[0]):
            for h in range(heads):
                q_rows[i * heads + h : i * heads + h + 1, :] = flat[i : i + 1, h * HD : (h + 1) * HD]
        mine[...] = q_rows[...].astype(jnp.bfloat16)
        anc[b, :, pl.ds(a * own_rows, own_rows), :] = kv[:, near:used]
        if used < kv.shape[1]:
            kv[:, used:] = jnp.zeros((2, kv.shape[1] - used, HD), jnp.bfloat16)
        loads[2].wait()
        length = len_ref[0]
        column = lax.broadcasted_iota(jnp.int32, bias.shape, 1)
        bias[...] = jnp.where(column < length, 0.0, NEG)
        column = lax.broadcasted_iota(jnp.int32, bias_col.shape, 0)
        hidden = ((column >= length) & (column < cached)) | (column >= used)
        bias_col[...] = jnp.where(hidden, NEG, 0.0)

        pl.semaphore_wait(barrier, 4 * (side - 1) + nt - 1)

        far_first = sorted(range(1, side), key=lambda k: -min(k, side - k))
        far_all = far_first + [0]

        def qa(k, owner):
            return rcopy(mine, qx.at[owner], QA, k, over_a(k))

        def qb_chunk(k, chunk):
            return rcopy(qx.at[chunk], q_all.at[a, chunk], QB, k, over_a(k))

        def qb(k, owner):
            return rcopy(qx, q_all.at[owner], QB, k, over_a(k))

        def all_of(x, ref, k=0, d=0):
            return rcopy(ref, ref, x, k, over_a(0), d)

        def ab(k, owner):
            place = anc.at[b, :, pl.ds(owner * own_rows, own_rows), :]
            return rcopy(place, place, AB, 0, on_a(k))

        def right(step, slot):
            place = anc.at[slot] if step < half else anc.at[slot, 0]
            return rcopy(place, place, AA, step - 1, on_b(1))

        def left(step, slot):
            place = anc.at[slot] if step < half else anc.at[slot, 1]
            return rcopy(place, place, AA, half + step - 1, on_b(side - 1))

        def slot_at(offset):
            return lax.rem(b + side + offset, side)

        def ring_send(step):
            if step <= half:
                right(step, slot_at(1 - step)).start()
                left(step, slot_at(step - 1)).start()

        def ring_send_on(core, step):
            @pl.when(par == core)
            def _():
                ring_send(step)

        def ring_recv(step):
            got = [slot_at(-step), slot_at(step)]
            right(step, got[0]).wait_recv()
            left(step, got[1]).wait_recv()
            if step == half:
                got = got[:1]
            return got

        for k in far_all:
            qa(k, a).start()

        group = min(heads, 4) * new_rows
        tri_row = lax.rem(lax.broadcasted_iota(jnp.int32, (group, new_rows), 0), new_rows)
        tri_col = lax.broadcasted_iota(jnp.int32, (group, new_rows), 1)

        def first_local(i, carry):
            r = pl.ds(pl.multiple_of(i * group, group), group)
            q = span_q[r, :]
            parts = [
                scores(q, kv[0, 0:cached]) + bias[0:1, :],
                jnp.where(tri_col <= tri_row, scores(q, kv[0, cached:near]), NEG),
            ]
            peak, total, o = lane_softmax(parts, [kv[1, 0:cached], kv[1, cached:near]])
            f_peak[r, :] = peak
            f_sum[r, :] = total
            f_out[r, :] = o
            return carry

        def first_anchor(slots, last=False):
            def body(i, carry):
                r = pl.ds(pl.multiple_of(i * group, group), group)
                q = span_q[r, :]
                parts = [scores(q, anc[s, 0]) for s in slots]
                before = f_peak[r, :]
                peak, total, o = lane_softmax(parts, [anc[s, 1] for s in slots], before)
                shrink = jnp.exp2((before - peak) * LOG2)
                total = f_sum[r, :] * shrink + total
                o = f_out[r, :] * shrink + o
                if last:
                    f_out[r, :] = o / jnp.sum(total, axis=1, keepdims=True)
                else:
                    f_peak[r, :] = peak
                    f_sum[r, :] = total
                    f_out[r, :] = o
                return carry

            lax.fori_loop(0, heads * new_rows // group, body, 0)

        for load in loads[3:6]:
            load.wait()
        pltpu.make_async_copy(span_q, span_q, in_sem.at[6]).wait()
        def forward(offsets):
            for d in offsets:
                chunk = back(b, d)
                qa(d, chunk).wait_recv()
                for k in far_all:
                    qb_chunk(k, chunk).start()

        values[...] = kv[1].T
        groups = heads * new_rows // group
        lax.fori_loop(0, (groups + 1) // 2, first_local, 0)
        for k in far_first:
            ab(k, a).start()
        forward([0] + sorted({1, side - 1}))
        for d in range(2, half + 1):
            forward(sorted({d, side - d}))
        def query_blocks(owners):
            q = [q_all[owner].reshape(rows, HD) for owner in owners]
            q = q[0] if len(q) == 1 else jnp.concatenate(q, axis=0)
            count = q.shape[0]
            w = scores(kv[0], q) + wide(bias_col[:, 0:rows], count)
            peak = jnp.max(w, axis=0, keepdims=True)
            w = jnp.exp2((w - peak) * LOG2)
            total = jnp.sum(w, axis=0, keepdims=True)
            o = jnp.dot(values[...], w.astype(jnp.bfloat16), preferred_element_type=jnp.float32)
            o = (o / total).astype(jnp.bfloat16)
            lse = peak * LOG2 + jnp.log2(total)
            for i, owner in enumerate(owners):
                ro_send[owner] = o[:, i * rows : (i + 1) * rows]
                rl_send[owner] = lse[:, i * rows : (i + 1) * rows]

        def ro_copy(k, block):
            return rcopy(ro_send.at[block], ro.at[par, b], RO, par, to_one(k))

        def rl_copy(k, block):
            return rcopy(rl_send.at[block], rl.at[par, b], RL, par, to_one(k))

        def some_blocks(offsets):
            owners = [back(b, k) for k in offsets]
            for k, owner in zip(offsets, owners):
                qb(k, owner).wait_recv()
            query_blocks(owners)
            for k, owner in zip(offsets, owners):
                if isinstance(k, int) and k == 0:

                    @pl.when(par == 1)
                    def _():
                        ro[1, b] = ro_send[b]
                        rl[1, b] = rl_send[b]

                    @pl.when(par == 0)
                    def _():
                        ro_copy(0, b).start()
                        rl_copy(0, b).start()

                else:
                    ro_copy(side - k, owner).start()
                    rl_copy(side - k, owner).start()

        some_blocks([0])

        all_of(AB, anc.at[b, :, pl.ds(0, (side - 1) * own_rows), :]).wait_recv()
        ring_send(1)


        def two_blocks(i, carry):
            some_blocks([half - i, half + i])
            return carry

        if half > 1:
            some_blocks([1, side - 1])
        some_blocks([half])
        lax.fori_loop(1, half - 1, two_blocks, 0)

        slots = [b] + ring_recv(1)
        ring_send_on(0, 2)
        lax.fori_loop((groups + 1) // 2, groups, first_local, 0)
        ring_send_on(1, 2)


        @pl.when(par == 0)
        def _():
            first_anchor(slots, last=half == 1)

        def combine(o_ref, l_ref, d):
            lse = [l_ref[d, i] for i in range(side)]
            peak = lse[0]
            for x in lse[1:]:
                peak = jnp.maximum(peak, x)
            weights = [jnp.exp2(x - peak) for x in lse]
            total = weights[0]
            for w in weights[1:]:
                total = total + w
            o = None
            for i in range(side):
                term = (weights[i] / total) * o_ref[d, i].astype(jnp.float32)
                o = term if o is None else o + term
            return o, peak + jnp.log2(total)

        def plane_slot(d):
            return a if d else b

        def plane_peer(d, k):
            return on_a(k) if d else on_b(k)

        def co_copy(d, k):
            place = co.at[d, plane_slot(d)]
            return rcopy(place, place, CO, d, plane_peer(d, k), d)

        def cl_copy(d, k):
            place = cl.at[d, plane_slot(d)]
            return rcopy(place, place, CL, d, plane_peer(d, k), d)

        def blocks_of(d):
            return slice(0, side - 1) if d else slice(0, side)


        @pl.when(par == 1)
        def _():
            for d in (1, 0):
                all_of(RO, ro.at[d, blocks_of(d)], d).wait_recv()
                all_of(RL, rl.at[d, blocks_of(d)], d).wait_recv()
                o, lse = combine(ro, rl, d)
                co[d, plane_slot(d)] = o.astype(jnp.bfloat16)
                cl[d, plane_slot(d)] = lse
                for k in far_first:
                    co_copy(d, k).start()
                    cl_copy(d, k).start()

        more = ring_recv(2) if half > 1 else []
        if more:

            @pl.when(par == 0)
            def _():
                first_anchor(more, last=half == 2)

        @pl.when(par == 1)
        def _():
            first_anchor(slots + more, last=half <= 2)

        ring_send(3)

        def gb(d, k):
            if d:
                return rcopy(done.at[1], att.at[b], GB, 0, on_b(k), d)
            return rcopy(done.at[0], att.at[a], GB, 0, over_a(k))


        @pl.when(par == 1)
        def _():
            for d in (1, 0):
                all_of(CO, co.at[d, 0 : side - 1], d).wait_recv()
                all_of(CL, cl.at[d, 0 : side - 1], d).wait_recv()
                o, _ = combine(co, cl, d)
                o = o.T.astype(jnp.bfloat16)
                done[d] = o
                for k in far_first if d else far_all:
                    gb(d, k).start()
                if d:
                    att[b] = o

        for step in range(3, half):
            slots = ring_recv(step)
            first_anchor(slots)
            ring_send(step + 1)

        for d in (0, 1):

            @pl.when(par == d)
            def _():
                all_of(GB, att.at[blocks_of(d)]).wait_recv()

        att_f[...] = att[...].reshape(-1, HD).astype(jnp.float32)
        count = att_f.shape[0] // heads
        per = count // ctx_count
        row = lax.broadcasted_iota(jnp.int32, (count, count), 0)
        col = lax.broadcasted_iota(jnp.int32, (count, count), 1)
        dev, sub = lax.div(row, per), lax.rem(row, per)
        swapped = (lax.rem(dev, side) * side + lax.div(dev, side)) * per + sub
        source = row + par * (swapped - row)
        perm = jnp.where(col == source, 1.0, 0.0).astype(jnp.bfloat16)
        total = None
        for h in range(heads):
            rows_h = att_f[pl.ds(h, count, stride=heads), :].astype(jnp.bfloat16)
            rows_h = jnp.dot(perm, rows_h, preferred_element_type=jnp.float32)
            term = jnp.dot(
                rows_h.astype(jnp.bfloat16), weight[h * HD : (h + 1) * HD, :],
                preferred_element_type=jnp.float32,
            )
            total = term if total is None else total + term
        proj[...] = total.reshape(proj.shape)
        tpr[t] = proj[t]

        def tp_copy(k, piece, owner):
            return rcopy(proj.at[piece], tpr.at[owner], TP, 0, on_t(k))

        for k in range(1, nt):
            tp_copy(k, lax.rem(t + k, nt), t).start()

        if half > 2:
            slots = ring_recv(half)
            first_anchor(slots, last=True)
        for h in range(heads):
            out[:, h * HD : (h + 1) * HD] = f_out[h * new_rows : (h + 1) * new_rows, :].astype(jnp.bfloat16)
        store = pltpu.make_async_copy(out, out_any, out_sem.at[0])
        store.start()

        all_of(TP, tpr.at[0 : nt - 1]).wait_recv()
        total = tpr[0]
        for i in range(1, nt):
            total = total + tpr[i]
        ans[...] = total.astype(jnp.bfloat16)
        final = pltpu.make_async_copy(ans, ans_any, out_sem.at[1])
        final.start()

        for x, ref in (
            (QA, qx), (QB, q_all), (AB, anc.at[b, :, pl.ds(0, (side - 1) * own_rows), :]),
            (AA, anc.at[0 : side - 1]), (TP, tpr.at[0 : nt - 1]),
        ):
            all_of(x, ref).wait_send()
        for d in (0, 1):

            @pl.when(par == d)
            def _():
                all_of(RO, ro_send.at[blocks_of(d)]).wait_send()
                all_of(RL, rl_send.at[blocks_of(d)]).wait_send()

        @pl.when(par == 1)
        def _():
            for d in (0, 1):
                all_of(CO, co.at[d, 0 : side - 1], d, d).wait_send()
                all_of(CL, cl.at[d, 0 : side - 1], d, d).wait_send()
                all_of(GB, att.at[blocks_of(d)], 0, d).wait_send()

        store.wait()
        final.wait()

    return kernel


def write_out(out_ref, ans_ref, out_hbm, ans_hbm, sem):
    copies = [
        pltpu.make_async_copy(out_ref, out_hbm, sem.at[0]),
        pltpu.make_async_copy(ans_ref, ans_hbm, sem.at[1]),
    ]
    for copy in copies:
        copy.start()
    for copy in copies:
        copy.wait()


def make_local(ctx_count, nt):
    side = math.isqrt(ctx_count)

    def local(span_q, span_kv, cache_kv, anchor_kv, block_len, queries, out_weight):
        new_rows = span_q.shape[0]
        heads = span_q.shape[1] // HD
        per = queries.shape[0]
        chunk = per * heads
        rows = side * chunk
        own = anchor_kv.shape[1]
        cols = out_weight.shape[1]
        keys = pl.cdiv(cache_kv.shape[1] + new_rows + own, HD) * HD
        answer_rows = per * ctx_count // nt
        any_spec = pl.BlockSpec(memory_space=pl.ANY)
        bf16, f32 = jnp.bfloat16, jnp.float32
        vmem = pltpu.VMEM
        results = pl.pallas_call(
            make_kernel(side, nt, heads),
            name="star",
            out_shape=(vmem(span_q.shape, bf16), vmem((answer_rows, cols), bf16)),
            in_specs=[pl.BlockSpec(memory_space=pltpu.HBM)] + [any_spec] * 6,
            out_specs=(any_spec, any_spec),
            scratch_shapes=[
                pltpu.SMEM(block_len.shape, jnp.int32),
                vmem((heads * new_rows, HD), bf16),
                vmem((2, keys, HD), bf16),
                vmem(queries.shape, bf16),
                vmem(out_weight.shape, bf16),
                vmem((chunk, HD), f32),
                vmem((8, cache_kv.shape[1]), f32),
                vmem((keys, HD), f32),
                vmem((HD, keys), bf16),
                vmem((chunk, HD), bf16),
                vmem((side, chunk, HD), bf16),
                vmem((side, side, chunk, HD), bf16),
                vmem((side, 2, side * own, HD), bf16),
                vmem((side, HD, rows), bf16),
                vmem((side, 1, rows), f32),
                vmem((2, side, HD, rows), bf16),
                vmem((2, side, 1, rows), f32),
                vmem((2, side, HD, rows), bf16),
                vmem((2, side, 1, rows), f32),
                vmem((2, rows, HD), bf16),
                vmem((side, rows, HD), bf16),
                vmem((side * rows, HD), f32),
                vmem((nt, answer_rows, cols), f32),
                vmem((nt, answer_rows, cols), f32),
                vmem((heads * new_rows, HD), f32),
                vmem((heads * new_rows, HD), f32),
                vmem((heads * new_rows, HD), f32),
                vmem(span_q.shape, bf16),
                vmem((answer_rows, cols), bf16),
                pltpu.SemaphoreType.DMA((7,)),
                pltpu.SemaphoreType.DMA((len(SENDS) + 3,)),
                pltpu.SemaphoreType.DMA((2 * len(SENDS) + 3 * (side - 2),)),
                pltpu.SemaphoreType.DMA((2,)),
            ],
            compiler_params=pltpu.CompilerParams(collective_id=0, has_side_effects=True),
        )(block_len, span_q, span_kv, cache_kv, anchor_kv, queries, out_weight)
        return pl.pallas_call(
            write_out,
            name="write",
            out_shape=[jax.ShapeDtypeStruct(x.shape, x.dtype) for x in results],
            in_specs=[pl.BlockSpec(memory_space=pltpu.VMEM)] * 2,
            out_specs=[any_spec, any_spec],
            scratch_shapes=[pltpu.SemaphoreType.DMA((2,))],
        )(*[pltpu.with_memory_space_constraint(x, pltpu.VMEM) for x in results])

    return local


def solution(mesh):
    placed = (
        P("ctx", "tp"),
        P(None, "ctx", "tp"),
        P(None, "ctx", "tp"),
        P(None, "ctx", "tp"),
        P("ctx"),
        P("ctx", "tp"),
        P("tp", "ctx"),
    )
    return jax.shard_map(
        make_local(mesh.shape["ctx"], mesh.shape["tp"]),
        mesh=mesh,
        in_specs=placed,
        out_specs=(P("ctx", "tp"), P("tp", "ctx")),
        check_vma=False,
    )
```

```python
import math

import jax
import jax.numpy as jnp
from jax import lax
from jax.experimental import pallas as pl
from jax.experimental.pallas import tpu as pltpu
from jax.sharding import PartitionSpec as P

HD = 128
NEG = -1e30
MESH = pl.DeviceIdType.MESH
LOG2 = math.log2(math.e) / math.sqrt(HD)

SENDS = QA, QB, AB, AA, RO, RL, CO, CL, GB, TP = range(10)


def scores(q, k):
    return lax.dot_general(q, k, (((1,), (1,)), ((), ())), preferred_element_type=jnp.float32)


def wide(x, columns):
    return x if columns == x.shape[1] else jnp.concatenate([x] * (columns // x.shape[1]), axis=1)


def lane_softmax(parts, values, before=None):
    top = None
    for s in parts:
        for c in range(0, s.shape[1], HD):
            piece = s[:, c : c + HD]
            top = piece if top is None else jnp.maximum(top, piece)
    peak = jnp.broadcast_to(jnp.max(top, axis=1, keepdims=True), top.shape)
    if before is not None:
        peak = jnp.maximum(peak, before)
    total, out = None, None
    for s, v in zip(parts, values):
        w = jnp.exp2((s - wide(peak, s.shape[1])) * LOG2)
        for c in range(0, w.shape[1], HD):
            piece = w[:, c : c + HD]
            total = piece if total is None else total + piece
        prod = jnp.dot(w.astype(jnp.bfloat16), v, preferred_element_type=jnp.float32)
        out = prod if out is None else out + prod
    return peak, total, out


def make_kernel(side, nt, heads):
    ctx_count = side * side
    half = side // 2

    def kernel(
        len_hbm, span_q_hbm, span_kv_hbm, cache_hbm, anchor_hbm, queries_hbm, weight_hbm,
        out_any, ans_any,
        len_ref, span_q, kv, queries, weight, q_rows, bias, bias_col, values,
        mine, qx, q_all, anc, ro_send, rl_send, ro, rl, co, cl, done, att, att_f, proj, tpr,
        f_peak, f_sum, f_out, out, ans,
        in_sem, ss, rs, out_sem,
    ):
        rows = q_all.shape[1] * q_all.shape[2]
        ctx = lax.axis_index("ctx")
        t = lax.axis_index("tp")
        par = lax.rem(t, 2)
        lo, hi = lax.rem(ctx, side), lax.div(ctx, side)
        a = lo + par * (hi - lo)
        b = hi + par * (lo - hi)

        other = t + 1 - 2 * par
        core_one = t + 1 - par

        def at(pa, pb, core):
            first = pb * side + pa
            return {"ctx": first + par * (pa * side + pb - first), "tp": core}

        def on_a(k):
            return at(lax.rem(a + k, side), b, t)

        def on_b(k):
            return at(a, lax.rem(b + k, side), t)

        def over_a(k):
            return at(lax.rem(a + k, side), b, other)

        def over_b(k):
            return at(a, lax.rem(b + k, side), other)

        def to_one(k):
            return at(a, lax.rem(b + k, side), core_one)

        def back(x, k):
            return lax.rem(x + side - k, side)

        def on_t(k):
            return {"tp": lax.rem(t + k, nt)}

        single = (QA, QB, AA)
        first_recv, used = {}, 0
        for x in SENDS:
            first_recv[x] = used
            used += side if x in single else 2

        second = {CO: len(SENDS), CL: len(SENDS) + 1, GB: len(SENDS) + 2}

        def rcopy(src, dst, x, k, dev, d=0):
            return pltpu.make_async_remote_copy(
                src_ref=src, dst_ref=dst, send_sem=ss.at[second[x] if d else x], recv_sem=rs.at[first_recv[x] + k],
                device_id=dev, device_id_type=MESH,
            )

        new_rows = out.shape[0]
        own_rows = anchor_hbm.shape[1]
        cached = cache_hbm.shape[1]
        near = cached + new_rows
        used = near + own_rows
        pairs = [
            (queries_hbm, queries), (anchor_hbm, kv.at[:, near:used]), (len_hbm, len_ref),
            (cache_hbm, kv.at[:, 0:cached]), (span_kv_hbm, kv.at[:, cached:near]), (weight_hbm, weight),
        ]
        for h in range(heads):
            pairs.append(
                (span_q_hbm.at[:, h * HD : (h + 1) * HD], span_q.at[h * new_rows : (h + 1) * new_rows])
            )
        loads = [
            pltpu.make_async_copy(src, dst, in_sem.at[min(i, 6)]) for i, (src, dst) in enumerate(pairs)
        ]
        barrier = pltpu.get_barrier_semaphore()
        for k in range(1, side):
            for peer in (on_a(k), on_b(k), over_a(k), over_b(k)):
                pl.semaphore_signal(barrier, inc=1, device_id=peer, device_id_type=MESH)
        for k in range(1, nt):
            pl.semaphore_signal(barrier, inc=1, device_id=on_t(k), device_id_type=MESH)

        for load in loads:
            load.start()

        loads[0].wait()
        loads[1].wait()
        flat = queries[...].astype(jnp.float32)
        for i in range(queries.shape[0]):
            for h in range(heads):
                q_rows[i * heads + h : i * heads + h + 1, :] = flat[i : i + 1, h * HD : (h + 1) * HD]
        mine[...] = q_rows[...].astype(jnp.bfloat16)
        anc[b, :, pl.ds(a * own_rows, own_rows), :] = kv[:, near:used]
        if used < kv.shape[1]:
            kv[:, used:] = jnp.zeros((2, kv.shape[1] - used, HD), jnp.bfloat16)
        loads[2].wait()
        length = len_ref[0]
        column = lax.broadcasted_iota(jnp.int32, bias.shape, 1)
        bias[...] = jnp.where(column < length, 0.0, NEG)
        column = lax.broadcasted_iota(jnp.int32, bias_col.shape, 0)
        hidden = ((column >= length) & (column < cached)) | (column >= used)
        bias_col[...] = jnp.where(hidden, NEG, 0.0)

        pl.semaphore_wait(barrier, 4 * (side - 1) + nt - 1)

        far_first = sorted(range(1, side), key=lambda k: -min(k, side - k))
        far_all = far_first + [0]

        def qa(k, owner):
            return rcopy(mine, qx.at[owner], QA, k, over_a(k))

        def qb_chunk(k, chunk):
            return rcopy(qx.at[chunk], q_all.at[a, chunk], QB, k, over_a(k))

        def qb(k, owner):
            return rcopy(qx, q_all.at[owner], QB, k, over_a(k))

        def all_of(x, ref, k=0, d=0):
            return rcopy(ref, ref, x, k, over_a(0), d)

        def ab(k, owner):
            place = anc.at[b, :, pl.ds(owner * own_rows, own_rows), :]
            return rcopy(place, place, AB, 0, on_a(k))

        def right(step, slot):
            place = anc.at[slot] if step < half else anc.at[slot, 0]
            return rcopy(place, place, AA, step - 1, on_b(1))

        def left(step, slot):
            place = anc.at[slot] if step < half else anc.at[slot, 1]
            return rcopy(place, place, AA, half + step - 1, on_b(side - 1))

        def slot_at(offset):
            return lax.rem(b + side + offset, side)

        def ring_send(step):
            if step <= half:
                right(step, slot_at(1 - step)).start()
                left(step, slot_at(step - 1)).start()

        def ring_send_on(core, step):
            @pl.when(par == core)
            def _():
                ring_send(step)

        def ring_recv(step):
            got = [slot_at(-step), slot_at(step)]
            right(step, got[0]).wait_recv()
            left(step, got[1]).wait_recv()
            if step == half:
                got = got[:1]
            return got

        for k in far_all:
            qa(k, a).start()

        group = min(heads, 4) * new_rows
        tri_row = lax.rem(lax.broadcasted_iota(jnp.int32, (group, new_rows), 0), new_rows)
        tri_col = lax.broadcasted_iota(jnp.int32, (group, new_rows), 1)

        def first_local(i, carry):
            r = pl.ds(pl.multiple_of(i * group, group), group)
            q = span_q[r, :]
            parts = [
                scores(q, kv[0, 0:cached]) + bias[0:1, :],
                jnp.where(tri_col <= tri_row, scores(q, kv[0, cached:near]), NEG),
            ]
            peak, total, o = lane_softmax(parts, [kv[1, 0:cached], kv[1, cached:near]])
            f_peak[r, :] = peak
            f_sum[r, :] = total
            f_out[r, :] = o
            return carry

        def first_anchor(slots, last=False):
            def body(i, carry):
                r = pl.ds(pl.multiple_of(i * group, group), group)
                q = span_q[r, :]
                parts = [scores(q, anc[s, 0]) for s in slots]
                before = f_peak[r, :]
                peak, total, o = lane_softmax(parts, [anc[s, 1] for s in slots], before)
                shrink = jnp.exp2((before - peak) * LOG2)
                total = f_sum[r, :] * shrink + total
                o = f_out[r, :] * shrink + o
                if last:
                    f_out[r, :] = o / jnp.sum(total, axis=1, keepdims=True)
                else:
                    f_peak[r, :] = peak
                    f_sum[r, :] = total
                    f_out[r, :] = o
                return carry

            lax.fori_loop(0, heads * new_rows // group, body, 0)

        for load in loads[3:6]:
            load.wait()
        pltpu.make_async_copy(span_q, span_q, in_sem.at[6]).wait()
        def forward(offsets):
            for d in offsets:
                chunk = back(b, d)
                qa(d, chunk).wait_recv()
                for k in far_all:
                    qb_chunk(k, chunk).start()

        values[...] = kv[1].T
        groups = heads * new_rows // group
        lax.fori_loop(0, (groups + 1) // 2, first_local, 0)
        for k in far_first:
            ab(k, a).start()
        forward([0] + sorted({1, side - 1}))
        for d in range(2, half + 1):
            forward(sorted({d, side - d}))
        def query_blocks(owners):
            q = [q_all[owner].reshape(rows, HD) for owner in owners]
            q = q[0] if len(q) == 1 else jnp.concatenate(q, axis=0)
            count = q.shape[0]
            w = scores(kv[0], q) + wide(bias_col[:, 0:rows], count)
            peak = jnp.max(w, axis=0, keepdims=True)
            w = jnp.exp2((w - peak) * LOG2)
            total = jnp.sum(w, axis=0, keepdims=True)
            o = jnp.dot(values[...], w.astype(jnp.bfloat16), preferred_element_type=jnp.float32)
            o = (o / total).astype(jnp.bfloat16)
            lse = peak * LOG2 + jnp.log2(total)
            for i, owner in enumerate(owners):
                ro_send[owner] = o[:, i * rows : (i + 1) * rows]
                rl_send[owner] = lse[:, i * rows : (i + 1) * rows]

        def ro_copy(k, block):
            return rcopy(ro_send.at[block], ro.at[par, b], RO, par, to_one(k))

        def rl_copy(k, block):
            return rcopy(rl_send.at[block], rl.at[par, b], RL, par, to_one(k))

        def some_blocks(offsets):
            owners = [back(b, k) for k in offsets]
            for k, owner in zip(offsets, owners):
                qb(k, owner).wait_recv()
            query_blocks(owners)
            for k, owner in zip(offsets, owners):
                if isinstance(k, int) and k == 0:

                    @pl.when(par == 1)
                    def _():
                        ro[1, b] = ro_send[b]
                        rl[1, b] = rl_send[b]

                    @pl.when(par == 0)
                    def _():
                        ro_copy(0, b).start()
                        rl_copy(0, b).start()

                else:
                    ro_copy(side - k, owner).start()
                    rl_copy(side - k, owner).start()

        some_blocks([0])

        all_of(AB, anc.at[b, :, pl.ds(0, (side - 1) * own_rows), :]).wait_recv()
        ring_send(1)


        def two_blocks(i, carry):
            some_blocks([half - i, half + i])
            return carry

        if half > 1:
            some_blocks([1, side - 1])
        some_blocks([half])
        lax.fori_loop(1, half - 1, two_blocks, 0)

        slots = [b] + ring_recv(1)
        ring_send_on(0, 2)
        lax.fori_loop((groups + 1) // 2, groups, first_local, 0)
        ring_send_on(1, 2)


        @pl.when(par == 0)
        def _():
            first_anchor(slots, last=half == 1)

        def combine(o_ref, l_ref, d):
            lse = [l_ref[d, i] for i in range(side)]
            peak = lse[0]
            for x in lse[1:]:
                peak = jnp.maximum(peak, x)
            weights = [jnp.exp2(x - peak) for x in lse]
            total = weights[0]
            for w in weights[1:]:
                total = total + w
            o = None
            for i in range(side):
                term = (weights[i] / total) * o_ref[d, i].astype(jnp.float32)
                o = term if o is None else o + term
            return o, peak + jnp.log2(total)

        def plane_slot(d):
            return a if d else b

        def plane_peer(d, k):
            return on_a(k) if d else on_b(k)

        def co_copy(d, k):
            place = co.at[d, plane_slot(d)]
            return rcopy(place, place, CO, d, plane_peer(d, k), d)

        def cl_copy(d, k):
            place = cl.at[d, plane_slot(d)]
            return rcopy(place, place, CL, d, plane_peer(d, k), d)

        def blocks_of(d):
            return slice(0, side - 1) if d else slice(0, side)


        @pl.when(par == 1)
        def _():
            for d in (1, 0):
                all_of(RO, ro.at[d, blocks_of(d)], d).wait_recv()
                all_of(RL, rl.at[d, blocks_of(d)], d).wait_recv()
                o, lse = combine(ro, rl, d)
                co[d, plane_slot(d)] = o.astype(jnp.bfloat16)
                cl[d, plane_slot(d)] = lse
                for k in far_first:
                    co_copy(d, k).start()
                    cl_copy(d, k).start()

        more = ring_recv(2) if half > 1 else []
        if more:

            @pl.when(par == 0)
            def _():
                first_anchor(more, last=half == 2)

        @pl.when(par == 1)
        def _():
            first_anchor(slots + more, last=half <= 2)

        ring_send(3)

        def gb(d, k):
            if d:
                return rcopy(done.at[1], att.at[b], GB, 0, on_b(k), d)
            return rcopy(done.at[0], att.at[a], GB, 0, over_a(k))


        @pl.when(par == 1)
        def _():
            for d in (0, 1):
                all_of(CO, co.at[d, 0 : side - 1], d).wait_recv()
                all_of(CL, cl.at[d, 0 : side - 1], d).wait_recv()
                o, _ = combine(co, cl, d)
                o = o.T.astype(jnp.bfloat16)
                done[d] = o
                for k in far_first if d else far_all:
                    gb(d, k).start()
                if d:
                    att[b] = o

        for step in range(3, half):
            slots = ring_recv(step)
            first_anchor(slots)
            ring_send(step + 1)

        for d in (0, 1):

            @pl.when(par == d)
            def _():
                all_of(GB, att.at[blocks_of(d)]).wait_recv()

        att_f[...] = att[...].reshape(-1, HD).astype(jnp.float32)
        count = att_f.shape[0] // heads
        total = None
        for h in range(heads):
            rows_h = att_f[pl.ds(h, count, stride=heads), :].astype(jnp.bfloat16)
            term = jnp.dot(
                rows_h, weight[h * HD : (h + 1) * HD, :], preferred_element_type=jnp.float32
            )
            total = term if total is None else total + term
        proj[...] = total.reshape(proj.shape)

        for d in (0, 1):

            @pl.when(par == d)
            def _():
                tpr[t] = proj[:, t] if d else proj[t]

        for d in (0, 1):

            @pl.when(par == d)
            def _():
                for k in range(1, nt):
                    piece = lax.rem(t + k, nt)
                    piece = proj.at[:, piece] if d else proj.at[piece]
                    rcopy(piece, tpr.at[t], TP, 0, on_t(k)).start()

        if half > 2:
            slots = ring_recv(half)
            first_anchor(slots, last=True)
        for h in range(heads):
            out[:, h * HD : (h + 1) * HD] = f_out[h * new_rows : (h + 1) * new_rows, :].astype(jnp.bfloat16)
        store = pltpu.make_async_copy(out, out_any, out_sem.at[0])
        store.start()

        all_of(TP, tpr.at[0 : nt - 1]).wait_recv()
        total = tpr[0]
        for i in range(1, nt):
            total = total + tpr[i]
        ans[...] = total.reshape(ans.shape).astype(jnp.bfloat16)
        final = pltpu.make_async_copy(ans, ans_any, out_sem.at[1])
        final.start()

        for x, ref in (
            (QA, qx), (QB, q_all), (AB, anc.at[b, :, pl.ds(0, (side - 1) * own_rows), :]),
            (AA, anc.at[0 : side - 1]), (TP, tpr.at[0 : nt - 1]),
        ):
            all_of(x, ref).wait_send()
        for d in (0, 1):

            @pl.when(par == d)
            def _():
                all_of(RO, ro_send.at[blocks_of(d)]).wait_send()
                all_of(RL, rl_send.at[blocks_of(d)]).wait_send()

        @pl.when(par == 1)
        def _():
            for d in (0, 1):
                all_of(CO, co.at[d, 0 : side - 1], d, d).wait_send()
                all_of(CL, cl.at[d, 0 : side - 1], d, d).wait_send()
                all_of(GB, att.at[blocks_of(d)], 0, d).wait_send()

        store.wait()
        final.wait()

    return kernel


def write_out(out_ref, ans_ref, out_hbm, ans_hbm, sem):
    copies = [
        pltpu.make_async_copy(out_ref, out_hbm, sem.at[0]),
        pltpu.make_async_copy(ans_ref, ans_hbm, sem.at[1]),
    ]
    for copy in copies:
        copy.start()
    for copy in copies:
        copy.wait()


def make_local(ctx_count, nt):
    side = math.isqrt(ctx_count)

    def local(span_q, span_kv, cache_kv, anchor_kv, block_len, queries, out_weight):
        new_rows = span_q.shape[0]
        heads = span_q.shape[1] // HD
        per = queries.shape[0]
        chunk = per * heads
        rows = side * chunk
        own = anchor_kv.shape[1]
        cols = out_weight.shape[1]
        keys = pl.cdiv(cache_kv.shape[1] + new_rows + own, HD) * HD
        answer_rows = per * ctx_count // nt
        any_spec = pl.BlockSpec(memory_space=pl.ANY)
        bf16, f32 = jnp.bfloat16, jnp.float32
        vmem = pltpu.VMEM
        results = pl.pallas_call(
            make_kernel(side, nt, heads),
            name="star",
            out_shape=(vmem(span_q.shape, bf16), vmem((answer_rows, cols), bf16)),
            in_specs=[pl.BlockSpec(memory_space=pltpu.HBM)] + [any_spec] * 6,
            out_specs=(any_spec, any_spec),
            scratch_shapes=[
                pltpu.SMEM(block_len.shape, jnp.int32),
                vmem((heads * new_rows, HD), bf16),
                vmem((2, keys, HD), bf16),
                vmem(queries.shape, bf16),
                vmem(out_weight.shape, bf16),
                vmem((chunk, HD), f32),
                vmem((8, cache_kv.shape[1]), f32),
                vmem((keys, HD), f32),
                vmem((HD, keys), bf16),
                vmem((chunk, HD), bf16),
                vmem((side, chunk, HD), bf16),
                vmem((side, side, chunk, HD), bf16),
                vmem((side, 2, side * own, HD), bf16),
                vmem((side, HD, rows), bf16),
                vmem((side, 1, rows), f32),
                vmem((2, side, HD, rows), bf16),
                vmem((2, side, 1, rows), f32),
                vmem((2, side, HD, rows), bf16),
                vmem((2, side, 1, rows), f32),
                vmem((2, rows, HD), bf16),
                vmem((side, rows, HD), bf16),
                vmem((side * rows, HD), f32),
                vmem((side, side, per, cols), f32),
                vmem((nt, side, per, cols), f32),
                vmem((heads * new_rows, HD), f32),
                vmem((heads * new_rows, HD), f32),
                vmem((heads * new_rows, HD), f32),
                vmem(span_q.shape, bf16),
                vmem((answer_rows, cols), bf16),
                pltpu.SemaphoreType.DMA((7,)),
                pltpu.SemaphoreType.DMA((len(SENDS) + 3,)),
                pltpu.SemaphoreType.DMA((2 * len(SENDS) + 3 * (side - 2),)),
                pltpu.SemaphoreType.DMA((2,)),
            ],
            compiler_params=pltpu.CompilerParams(collective_id=0, has_side_effects=True),
        )(block_len, span_q, span_kv, cache_kv, anchor_kv, queries, out_weight)
        return pl.pallas_call(
            write_out,
            name="write",
            out_shape=[jax.ShapeDtypeStruct(x.shape, x.dtype) for x in results],
            in_specs=[pl.BlockSpec(memory_space=pltpu.VMEM)] * 2,
            out_specs=[any_spec, any_spec],
            scratch_shapes=[pltpu.SemaphoreType.DMA((2,))],
        )(*[pltpu.with_memory_space_constraint(x, pltpu.VMEM) for x in results])

    return local


def solution(mesh):
    placed = (
        P("ctx", "tp"),
        P(None, "ctx", "tp"),
        P(None, "ctx", "tp"),
        P(None, "ctx", "tp"),
        P("ctx"),
        P("ctx", "tp"),
        P("tp", "ctx"),
    )
    return jax.shard_map(
        make_local(mesh.shape["ctx"], mesh.shape["tp"]),
        mesh=mesh,
        in_specs=placed,
        out_specs=(P("ctx", "tp"), P("tp", "ctx")),
        check_vma=False,
    )
```

```python
import math

import jax
import jax.numpy as jnp
from jax import lax
from jax.experimental import pallas as pl
from jax.experimental.pallas import tpu as pltpu
from jax.sharding import PartitionSpec as P

HD = 128
NEG = -1e30
MESH = pl.DeviceIdType.MESH
LOG2 = math.log2(math.e) / math.sqrt(HD)

SENDS = QA, QB, AB, AA, RO, RL, CO, CL, GB, TP = range(10)


def scores(q, k):
    return lax.dot_general(q, k, (((1,), (1,)), ((), ())), preferred_element_type=jnp.float32)


def wide(x, columns):
    return x if columns == x.shape[1] else jnp.concatenate([x] * (columns // x.shape[1]), axis=1)


def lane_softmax(parts, values, before=None):
    top = None
    for s in parts:
        for c in range(0, s.shape[1], HD):
            piece = s[:, c : c + HD]
            top = piece if top is None else jnp.maximum(top, piece)
    peak = jnp.broadcast_to(jnp.max(top, axis=1, keepdims=True), top.shape)
    if before is not None:
        peak = jnp.maximum(peak, before)
    total, out = None, None
    for s, v in zip(parts, values):
        w = jnp.exp2((s - wide(peak, s.shape[1])) * LOG2)
        for c in range(0, w.shape[1], HD):
            piece = w[:, c : c + HD]
            total = piece if total is None else total + piece
        prod = jnp.dot(w.astype(jnp.bfloat16), v, preferred_element_type=jnp.float32)
        out = prod if out is None else out + prod
    return peak, total, out


def make_kernel(side, nt, heads):
    ctx_count = side * side
    half = side // 2

    def kernel(
        len_hbm, span_q_hbm, span_kv_hbm, cache_hbm, anchor_hbm, queries_hbm, weight_hbm,
        out_any, ans_any,
        len_ref, span_q, kv, queries, weight, q_rows, bias, bias_col, values,
        mine, qx, q_all, anc, ro_send, rl_send, ro, rl, co, cl, done, att, att_f, proj, tpr,
        f_peak, f_sum, f_out, out, ans,
        in_sem, ss, rs, out_sem,
    ):
        rows = q_all.shape[1] * q_all.shape[2]
        ctx = lax.axis_index("ctx")
        t = lax.axis_index("tp")
        par = lax.rem(t, 2)
        lo, hi = lax.rem(ctx, side), lax.div(ctx, side)
        a = lo + par * (hi - lo)
        b = hi + par * (lo - hi)

        other = t + 1 - 2 * par
        core_one = t + 1 - par

        def at(pa, pb, core):
            first = pb * side + pa
            return {"ctx": first + par * (pa * side + pb - first), "tp": core}

        def on_a(k):
            return at(lax.rem(a + k, side), b, t)

        def on_b(k):
            return at(a, lax.rem(b + k, side), t)

        def over_a(k):
            return at(lax.rem(a + k, side), b, other)

        def over_b(k):
            return at(a, lax.rem(b + k, side), other)

        def to_one(k):
            return at(a, lax.rem(b + k, side), core_one)

        def back(x, k):
            return lax.rem(x + side - k, side)

        def on_t(k):
            return {"tp": lax.rem(t + k, nt)}

        single = (QA, QB, AA)
        first_recv, used = {}, 0
        for x in SENDS:
            first_recv[x] = used
            used += side if x in single else 2 if x in (RO, RL, CO, CL) else 1

        second = {CO: len(SENDS), CL: len(SENDS) + 1, GB: len(SENDS) + 2}

        def rcopy(src, dst, x, k, dev, d=0):
            return pltpu.make_async_remote_copy(
                src_ref=src, dst_ref=dst, send_sem=ss.at[second[x] if d else x], recv_sem=rs.at[first_recv[x] + k],
                device_id=dev, device_id_type=MESH,
            )

        new_rows = out.shape[0]
        own_rows = anchor_hbm.shape[1]
        cached = cache_hbm.shape[1]
        near = cached + new_rows
        used = near + own_rows
        pairs = [
            (queries_hbm, queries), (anchor_hbm, kv.at[:, near:used]), (len_hbm, len_ref),
            (cache_hbm, kv.at[:, 0:cached]), (span_kv_hbm, kv.at[:, cached:near]), (weight_hbm, weight),
        ]
        for h in range(heads):
            pairs.append(
                (span_q_hbm.at[:, h * HD : (h + 1) * HD], span_q.at[h * new_rows : (h + 1) * new_rows])
            )
        loads = [
            pltpu.make_async_copy(src, dst, in_sem.at[min(i, 6)]) for i, (src, dst) in enumerate(pairs)
        ]
        barrier = pltpu.get_barrier_semaphore()
        for k in range(1, side):
            for peer in (on_a(k), on_b(k), over_a(k), over_b(k)):
                pl.semaphore_signal(barrier, inc=1, device_id=peer, device_id_type=MESH)
        for k in range(1, nt):
            pl.semaphore_signal(barrier, inc=1, device_id=on_t(k), device_id_type=MESH)

        for load in loads:
            load.start()

        loads[0].wait()
        loads[1].wait()
        flat = queries[...].astype(jnp.float32)
        for i in range(queries.shape[0]):
            for h in range(heads):
                q_rows[i * heads + h : i * heads + h + 1, :] = flat[i : i + 1, h * HD : (h + 1) * HD]
        mine[...] = q_rows[...].astype(jnp.bfloat16)
        anc[b, :, pl.ds(a * own_rows, own_rows), :] = kv[:, near:used]
        if used < kv.shape[1]:
            kv[:, used:] = jnp.zeros((2, kv.shape[1] - used, HD), jnp.bfloat16)
        loads[2].wait()
        length = len_ref[0]
        column = lax.broadcasted_iota(jnp.int32, bias.shape, 1)
        bias[...] = jnp.where(column < length, 0.0, NEG)
        column = lax.broadcasted_iota(jnp.int32, bias_col.shape, 0)
        hidden = ((column >= length) & (column < cached)) | (column >= used)
        bias_col[...] = jnp.where(hidden, NEG, 0.0)

        pl.semaphore_wait(barrier, 4 * (side - 1) + nt - 1)

        far_first = sorted(range(1, side), key=lambda k: -min(k, side - k))
        far_all = far_first + [0]

        def qa(k, owner):
            return rcopy(mine, qx.at[owner], QA, k, over_a(k))

        def qb_chunk(k, chunk):
            return rcopy(qx.at[chunk], q_all.at[a, chunk], QB, k, over_a(k))

        def qb(k, owner):
            return rcopy(qx, q_all.at[owner], QB, k, over_a(k))

        def all_of(x, ref, k=0, d=0):
            return rcopy(ref, ref, x, k, over_a(0), d)

        def ab(k, owner):
            place = anc.at[b, :, pl.ds(owner * own_rows, own_rows), :]
            return rcopy(place, place, AB, 0, on_a(k))

        def right(step, slot):
            place = anc.at[slot] if step < half else anc.at[slot, 0]
            return rcopy(place, place, AA, step - 1, on_b(1))

        def left(step, slot):
            place = anc.at[slot] if step < half else anc.at[slot, 1]
            return rcopy(place, place, AA, half + step - 1, on_b(side - 1))

        def slot_at(offset):
            return lax.rem(b + side + offset, side)

        def ring_send(step):
            if step <= half:
                right(step, slot_at(1 - step)).start()
                left(step, slot_at(step - 1)).start()

        def ring_send_on(core, step):
            @pl.when(par == core)
            def _():
                ring_send(step)

        def ring_recv(step):
            got = [slot_at(-step), slot_at(step)]
            right(step, got[0]).wait_recv()
            left(step, got[1]).wait_recv()
            if step == half:
                got = got[:1]
            return got

        for k in far_all:
            qa(k, a).start()

        group = min(heads, 4) * new_rows
        tri_row = lax.rem(lax.broadcasted_iota(jnp.int32, (group, new_rows), 0), new_rows)
        tri_col = lax.broadcasted_iota(jnp.int32, (group, new_rows), 1)

        def first_local(i, carry):
            r = pl.ds(pl.multiple_of(i * group, group), group)
            q = span_q[r, :]
            parts = [
                scores(q, kv[0, 0:cached]) + bias[0:1, :],
                jnp.where(tri_col <= tri_row, scores(q, kv[0, cached:near]), NEG),
            ]
            peak, total, o = lane_softmax(parts, [kv[1, 0:cached], kv[1, cached:near]])
            f_peak[r, :] = peak
            f_sum[r, :] = total
            f_out[r, :] = o
            return carry

        def first_anchor(slots, last=False):
            def body(i, carry):
                r = pl.ds(pl.multiple_of(i * group, group), group)
                q = span_q[r, :]
                parts = [scores(q, anc[s, 0]) for s in slots]
                before = f_peak[r, :]
                peak, total, o = lane_softmax(parts, [anc[s, 1] for s in slots], before)
                shrink = jnp.exp2((before - peak) * LOG2)
                total = f_sum[r, :] * shrink + total
                o = f_out[r, :] * shrink + o
                if last:
                    f_out[r, :] = o / jnp.sum(total, axis=1, keepdims=True)
                else:
                    f_peak[r, :] = peak
                    f_sum[r, :] = total
                    f_out[r, :] = o
                return carry

            lax.fori_loop(0, heads * new_rows // group, body, 0)

        for load in loads[3:6]:
            load.wait()
        pltpu.make_async_copy(span_q, span_q, in_sem.at[6]).wait()
        def forward(offsets):
            for d in offsets:
                chunk = back(b, d)
                qa(d, chunk).wait_recv()
                for k in far_all:
                    qb_chunk(k, chunk).start()

        values[...] = kv[1].T
        groups = heads * new_rows // group
        lax.fori_loop(0, (groups + 1) // 2, first_local, 0)
        for k in far_first:
            ab(k, a).start()
        forward([0] + sorted({1, side - 1}))
        for d in range(2, half + 1):
            forward(sorted({d, side - d}))
        def query_blocks(owners):
            q = [q_all[owner].reshape(rows, HD) for owner in owners]
            q = q[0] if len(q) == 1 else jnp.concatenate(q, axis=0)
            count = q.shape[0]
            w = scores(kv[0], q) + wide(bias_col[:, 0:rows], count)
            peak = jnp.max(w, axis=0, keepdims=True)
            w = jnp.exp2((w - peak) * LOG2)
            total = jnp.sum(w, axis=0, keepdims=True)
            o = jnp.dot(values[...], w.astype(jnp.bfloat16), preferred_element_type=jnp.float32)
            o = (o / total).astype(jnp.bfloat16)
            lse = peak * LOG2 + jnp.log2(total)
            for i, owner in enumerate(owners):
                ro_send[owner] = o[:, i * rows : (i + 1) * rows]
                rl_send[owner] = lse[:, i * rows : (i + 1) * rows]

        def ro_copy(k, block):
            return rcopy(ro_send.at[block], ro.at[par, b], RO, par, to_one(k))

        def rl_copy(k, block):
            return rcopy(rl_send.at[block], rl.at[par, b], RL, par, to_one(k))

        def some_blocks(offsets):
            owners = [back(b, k) for k in offsets]
            for k, owner in zip(offsets, owners):
                qb(k, owner).wait_recv()
            query_blocks(owners)
            for k, owner in zip(offsets, owners):
                if isinstance(k, int) and k == 0:

                    @pl.when(par == 1)
                    def _():
                        ro[1, b] = ro_send[b]
                        rl[1, b] = rl_send[b]

                    @pl.when(par == 0)
                    def _():
                        ro_copy(0, b).start()
                        rl_copy(0, b).start()

                else:
                    ro_copy(side - k, owner).start()
                    rl_copy(side - k, owner).start()

        some_blocks([0])

        all_of(AB, anc.at[b, :, pl.ds(0, (side - 1) * own_rows), :]).wait_recv()
        ring_send(1)


        if half > 1:
            some_blocks([1, side - 1])
        some_blocks([half])
        rest = [k for i in range(1, half - 1) for k in (half - i, half + i)]
        if rest:
            some_blocks(rest)

        slots = [b] + ring_recv(1)
        ring_send_on(0, 2)
        lax.fori_loop((groups + 1) // 2, groups, first_local, 0)
        ring_send_on(1, 2)


        @pl.when(par == 0)
        def _():
            first_anchor(slots, last=half == 1)

        def combine(o_ref, l_ref, d):
            lse = [l_ref[d, i] for i in range(side)]
            peak = lse[0]
            for x in lse[1:]:
                peak = jnp.maximum(peak, x)
            weights = [jnp.exp2(x - peak) for x in lse]
            total = weights[0]
            for w in weights[1:]:
                total = total + w
            o = None
            for i in range(side):
                term = (weights[i] / total) * o_ref[d, i].astype(jnp.float32)
                o = term if o is None else o + term
            return o, peak + jnp.log2(total)

        def plane_slot(d):
            return a if d else b

        def plane_peer(d, k):
            return on_a(k) if d else on_b(k)

        def co_copy(d, k):
            place = co.at[d, plane_slot(d)]
            return rcopy(place, place, CO, d, plane_peer(d, k), d)

        def cl_copy(d, k):
            place = cl.at[d, plane_slot(d)]
            return rcopy(place, place, CL, d, plane_peer(d, k), d)

        def blocks_of(d):
            return slice(0, side - 1) if d else slice(0, side)


        @pl.when(par == 1)
        def _():
            for d in (1, 0):
                all_of(RO, ro.at[d, blocks_of(d)], d).wait_recv()
                all_of(RL, rl.at[d, blocks_of(d)], d).wait_recv()
                o, lse = combine(ro, rl, d)
                co[d, plane_slot(d)] = o.astype(jnp.bfloat16)
                cl[d, plane_slot(d)] = lse
                for k in far_first:
                    co_copy(d, k).start()
                    cl_copy(d, k).start()

        more = ring_recv(2) if half > 1 else []
        if more:

            @pl.when(par == 0)
            def _():
                first_anchor(more, last=half == 2)

        @pl.when(par == 1)
        def _():
            first_anchor(slots + more, last=half <= 2)

        ring_send(3)

        def gb(d, k):
            if d:
                return rcopy(done.at[1], att.at[b], GB, 0, on_b(k), d)
            return rcopy(done.at[0], att.at[a], GB, 0, over_a(k))


        @pl.when(par == 1)
        def _():
            for d in (0, 1):
                all_of(CO, co.at[d, 0 : side - 1], d).wait_recv()
                all_of(CL, cl.at[d, 0 : side - 1], d).wait_recv()
                o, _ = combine(co, cl, d)
                o = o.T.astype(jnp.bfloat16)
                done[d] = o
                for k in far_first if d else far_all:
                    gb(d, k).start()
                if d:
                    att[b] = o

        for step in range(3, half):
            slots = ring_recv(step)
            first_anchor(slots)
            ring_send(step + 1)

        for d in (0, 1):

            @pl.when(par == d)
            def _():
                all_of(GB, att.at[blocks_of(d)]).wait_recv()

        att_f[...] = att[...].reshape(-1, HD).astype(jnp.float32)
        count = att_f.shape[0] // heads
        total = None
        for h in range(heads):
            rows_h = att_f[pl.ds(h, count, stride=heads), :].astype(jnp.bfloat16)
            term = jnp.dot(
                rows_h, weight[h * HD : (h + 1) * HD, :], preferred_element_type=jnp.float32
            )
            total = term if total is None else total + term
        proj[...] = total.reshape(proj.shape)

        for d in (0, 1):

            @pl.when(par == d)
            def _():
                tpr[t] = proj[:, t] if d else proj[t]

        for d in (0, 1):

            @pl.when(par == d)
            def _():
                for k in range(1, nt):
                    piece = lax.rem(t + k, nt)
                    piece = proj.at[:, piece] if d else proj.at[piece]
                    rcopy(piece, tpr.at[t], TP, 0, on_t(k)).start()

        if half > 2:
            slots = ring_recv(half)
            first_anchor(slots, last=True)
        for h in range(heads):
            out[:, h * HD : (h + 1) * HD] = f_out[h * new_rows : (h + 1) * new_rows, :].astype(jnp.bfloat16)
        store = pltpu.make_async_copy(out, out_any, out_sem.at[0])
        store.start()

        all_of(TP, tpr.at[0 : nt - 1]).wait_recv()
        total = tpr[0]
        for i in range(1, nt):
            total = total + tpr[i]
        ans[...] = total.reshape(ans.shape).astype(jnp.bfloat16)
        final = pltpu.make_async_copy(ans, ans_any, out_sem.at[1])
        final.start()

        for x, ref in (
            (QA, qx), (QB, q_all), (AB, anc.at[b, :, pl.ds(0, (side - 1) * own_rows), :]),
            (AA, anc.at[0 : side - 1]), (TP, tpr.at[0 : nt - 1]),
        ):
            all_of(x, ref).wait_send()
        for d in (0, 1):

            @pl.when(par == d)
            def _():
                all_of(RO, ro_send.at[blocks_of(d)]).wait_send()
                all_of(RL, rl_send.at[blocks_of(d)]).wait_send()

        @pl.when(par == 1)
        def _():
            for d in (0, 1):
                all_of(CO, co.at[d, 0 : side - 1], d, d).wait_send()
                all_of(CL, cl.at[d, 0 : side - 1], d, d).wait_send()
                all_of(GB, att.at[blocks_of(d)], 0, d).wait_send()

        store.wait()
        final.wait()

    return kernel


def write_out(out_ref, ans_ref, out_hbm, ans_hbm, sem):
    copies = [
        pltpu.make_async_copy(out_ref, out_hbm, sem.at[0]),
        pltpu.make_async_copy(ans_ref, ans_hbm, sem.at[1]),
    ]
    for copy in copies:
        copy.start()
    for copy in copies:
        copy.wait()


def make_local(ctx_count, nt):
    side = math.isqrt(ctx_count)

    def local(span_q, span_kv, cache_kv, anchor_kv, block_len, queries, out_weight):
        new_rows = span_q.shape[0]
        heads = span_q.shape[1] // HD
        per = queries.shape[0]
        chunk = per * heads
        rows = side * chunk
        own = anchor_kv.shape[1]
        cols = out_weight.shape[1]
        keys = pl.cdiv(cache_kv.shape[1] + new_rows + own, HD) * HD
        answer_rows = per * ctx_count // nt
        any_spec = pl.BlockSpec(memory_space=pl.ANY)
        bf16, f32 = jnp.bfloat16, jnp.float32
        vmem = pltpu.VMEM
        results = pl.pallas_call(
            make_kernel(side, nt, heads),
            name="star",
            out_shape=(vmem(span_q.shape, bf16), vmem((answer_rows, cols), bf16)),
            in_specs=[pl.BlockSpec(memory_space=pltpu.HBM)] + [any_spec] * 6,
            out_specs=(any_spec, any_spec),
            scratch_shapes=[
                pltpu.SMEM(block_len.shape, jnp.int32),
                vmem((heads * new_rows, HD), bf16),
                vmem((2, keys, HD), bf16),
                vmem(queries.shape, bf16),
                vmem(out_weight.shape, bf16),
                vmem((chunk, HD), f32),
                vmem((8, cache_kv.shape[1]), f32),
                vmem((keys, HD), f32),
                vmem((HD, keys), bf16),
                vmem((chunk, HD), bf16),
                vmem((side, chunk, HD), bf16),
                vmem((side, side, chunk, HD), bf16),
                vmem((side, 2, side * own, HD), bf16),
                vmem((side, HD, rows), bf16),
                vmem((side, 1, rows), f32),
                vmem((2, side, HD, rows), bf16),
                vmem((2, side, 1, rows), f32),
                vmem((2, side, HD, rows), bf16),
                vmem((2, side, 1, rows), f32),
                vmem((2, rows, HD), bf16),
                vmem((side, rows, HD), bf16),
                vmem((side * rows, HD), f32),
                vmem((side, side, per, cols), f32),
                vmem((nt, side, per, cols), f32),
                vmem((heads * new_rows, HD), f32),
                vmem((heads * new_rows, HD), f32),
                vmem((heads * new_rows, HD), f32),
                vmem(span_q.shape, bf16),
                vmem((answer_rows, cols), bf16),
                pltpu.SemaphoreType.DMA((7,)),
                pltpu.SemaphoreType.DMA((len(SENDS) + 3,)),
                pltpu.SemaphoreType.DMA((len(SENDS) + 4 + 3 * (side - 1),)),
                pltpu.SemaphoreType.DMA((2,)),
            ],
            compiler_params=pltpu.CompilerParams(collective_id=0, has_side_effects=True),
        )(block_len, span_q, span_kv, cache_kv, anchor_kv, queries, out_weight)
        return pl.pallas_call(
            write_out,
            name="write",
            out_shape=[jax.ShapeDtypeStruct(x.shape, x.dtype) for x in results],
            in_specs=[pl.BlockSpec(memory_space=pltpu.VMEM)] * 2,
            out_specs=[any_spec, any_spec],
            scratch_shapes=[pltpu.SemaphoreType.DMA((2,))],
        )(*[pltpu.with_memory_space_constraint(x, pltpu.VMEM) for x in results])

    return local


def solution(mesh):
    placed = (
        P("ctx", "tp"),
        P(None, "ctx", "tp"),
        P(None, "ctx", "tp"),
        P(None, "ctx", "tp"),
        P("ctx"),
        P("ctx", "tp"),
        P("tp", "ctx"),
    )
    return jax.shard_map(
        make_local(mesh.shape["ctx"], mesh.shape["tp"]),
        mesh=mesh,
        in_specs=placed,
        out_specs=(P("ctx", "tp"), P("tp", "ctx")),
        check_vma=False,
    )
```
